32 devices in a mesh: gx: 2 (over y), gy: 16 (over z, x, core).
Axes of the slice: x: 2, y: 2, z: 4, core: 2. Of those that a mesh axis runs over, the one named last changes fastest.
Arguments:
- agents: bfloat16 [4, 64, 128, 256], P('gx', 'gy'), may hold values from -14 to 14
- block_fill: int32 [4, 64], replicated, may hold values from 64 to 96, as said below
- neighbours: int32 [4, 64, 4], P('gx', 'gy'), may hold values from 0 to 23, all different within a row
- target_slot: int32 [4, 64, 128], P('gx', 'gy'), may hold values from -1 to 1535, as said below
- attention_in: bfloat16 [256, 768], replicated, may hold values from -0.375 to 0.375
- attention_out: bfloat16 [256, 256], replicated, may hold values from -0.375 to 0.375
- policy_in: bfloat16 [512, 1024], replicated, may hold values from -0.25 to 0.25
- policy_mid: bfloat16 [2, 1024, 1024], replicated, may hold values from -0.1875 to 0.1875
- policy_out: bfloat16 [1024, 128], replicated, may hold values from -0.1875 to 0.1875
Outputs:
- actions: bfloat16 [4, 64, 128, 128], P('gx', 'gy')
- batch_obs: bfloat16 [2, 16, 768, 512], P('gx', 'gy')
The draws below stay inside these ranges and needn't reach their ends.
Inputs may be any that keep to these rules, and one draw needn't show every extreme that they name: The live slots of a block are its first block_fill ones; a tile holds at most 768 live agents. `neighbours`: the 4 directions of a block are distinct; direction d numbers the offsets (dx, dy) with -2 <= dx, dy <= 2 other than (0, 0) in row-major order. `target_slot`: -1 exactly for the slots at or beyond their block's fill; a live slot in a block of x index i holds o * 768 + (i // 2) * 384 + r with an owner o and 0 <= r < 384, and no two slots of one tile hold the same value.
All inputs are finite; a program needn't handle non-finite values.
Results may differ from the reference program's by a relative error of at most 0.0079.
Values may be sent and summed in bfloat16 or wider, within the bound.
No kernel may reach another device: no remote copies, remote signals or barrier semaphores. Data moves between devices by JAX's collectives and lax.ppermute only.
A program may use at most 64 MiB of HBM per device.

```python
import math
import jax
import jax.numpy as jnp
from jax import lax

F = 256
HEADS = 4
BLK = 128
NBR = 4
HID = 1024
MID = 2
ACT = 128
BX = 2
BY = 4
NXB = 4
NYB = 64
OWNERS = 2
TILE_ROWS = 16
A_DEV = 1024
CAP = 384
BATCH = 768
N_GX = 2
N_GY = 16


def fill_table(key):
    key_level, key_raw, key_full_x, key_full_y = jax.random.split(jax.random.fold_in(key, 11), 4)
    tile_level = jax.random.randint(key_level, (OWNERS, TILE_ROWS), 1, 5)
    tile_level = jnp.repeat(jnp.repeat(tile_level, BX, axis=0), BY, axis=1)
    raw_fill = jax.random.randint(key_raw, (NXB, NYB), 0, 2 * BLK)
    fill_now = jnp.clip(raw_fill * tile_level // 4, BLK // OWNERS, 3 * BLK // 4)
    tile_x = jax.random.randint(key_full_x, (), 0, OWNERS)
    tile_y = jax.random.randint(key_full_y, (), 0, TILE_ROWS)
    full_tile = jnp.full((BX, BY), 3 * BLK // 4, jnp.int32)
    fill_now = lax.dynamic_update_slice(fill_now.astype(jnp.int32), full_tile, (tile_x * BX, tile_y * BY))
    fill_now = fill_now.at[(tile_x + 1) % OWNERS * BX, tile_y * BY].set(BLK // OWNERS)
    return fill_now.astype(jnp.int32)


def draw_block_fill(key, part):
    return fill_table(key)


def draw_target_slot(key, part):
    fill_now = fill_table(key)
    key_order, key_shift = jax.random.split(jax.random.fold_in(key, 23))
    tiles_y = TILE_ROWS
    slot_index = jnp.arange(BLK, dtype=jnp.int32)
    live_slots = slot_index[None, None, :] < fill_now[:, :, None]
    tile_live = live_slots.reshape(OWNERS, BX, tiles_y, BY, BLK).transpose(0, 2, 1, 3, 4).reshape(OWNERS, tiles_y, A_DEV)
    local_index = jnp.arange(A_DEV, dtype=jnp.int32)
    noise_draw = jax.random.randint(key_order, (OWNERS, tiles_y, A_DEV), 0, 2 ** 29 // A_DEV)
    scores = noise_draw * A_DEV + local_index + jnp.where(tile_live, 0, 2 ** 30)
    sort_order = jnp.argsort(scores, axis=-1)
    live_rank = jnp.argsort(sort_order, axis=-1).astype(jnp.int32)
    owner_shift = jax.random.randint(key_shift, (), 0, OWNERS)
    source = jnp.arange(OWNERS, dtype=jnp.int32)[:, None, None]
    owner_index = (live_rank + source + owner_shift) % OWNERS
    target = owner_index * BATCH + source * CAP + live_rank // OWNERS
    target = jnp.where(tile_live, target, -1)
    target = target.reshape(OWNERS, tiles_y, BX, BY, BLK).transpose(0, 2, 1, 3, 4).reshape(NXB, NYB, BLK)
    return target.astype(jnp.int32)


def draw_agents(key, part):
    key_base, key_scale = jax.random.split(jax.random.fold_in(key, 37), 2)
    full_shape = (NXB, NYB, BLK, F)
    base_draw = jnp.clip(jax.random.normal(key_base, full_shape, jnp.float32), -4.0, 4.0)
    row_scale = jnp.exp(jax.random.uniform(key_scale, (NXB, NYB, BLK, 1), jnp.float32, -1.2, 1.2))
    return (base_draw * row_scale).astype(jnp.bfloat16)


def picks_of(rng, rows, count, top, lift):
    order = jax.random.permutation(jax.random.fold_in(rng, 1), count)
    pull = order
    for power in range(3):
        pull = pull * pull // count
    pull = pull * lift // count
    chance = jax.random.randint(jax.random.fold_in(rng, 2), (rows, count), 0, 4096) + pull
    sure = jax.random.permutation(jax.random.fold_in(rng, 3), rows)[jnp.arange(count) % rows]
    chance = jnp.where(jnp.arange(rows)[:, None] == sure[None, :], 1 << 14, chance)
    priority = chance * count + jnp.arange(count)
    return lax.top_k(priority.astype(jnp.int32), top)[1].astype(jnp.int32)


def normal_values(key, extent, spread, most, held_as=jnp.bfloat16):
    values = spread * jax.random.normal(key, extent, jnp.float32)
    return jnp.clip(values, min=-most, max=most).astype(held_as)


def setup_inputs(seed: int = 0) -> dict:
    streams_of = jax.random.split(jax.random.key(seed), 10)
    return {
        "agents": draw_agents(jax.random.fold_in(streams_of[9], 71), 0),
        "block_fill": draw_block_fill(jax.random.fold_in(streams_of[9], 71), 0),
        "neighbours": picks_of(streams_of[2], NXB * NYB, 24, NBR, 0).reshape((NXB, NYB, NBR)),
        "target_slot": draw_target_slot(jax.random.fold_in(streams_of[9], 71), 0),
        "attention_in": normal_values(streams_of[4], (F, 3 * F), F ** -0.5, 0.375),
        "attention_out": normal_values(streams_of[5], (F, F), F ** -0.5, 0.375),
        "policy_in": normal_values(streams_of[6], (2 * F, HID), (2 * F) ** -0.5, 0.25),
        "policy_mid": normal_values(streams_of[7], (MID, HID, HID), HID ** -0.5, 0.1875),
        "policy_out": normal_values(streams_of[8], (HID, ACT), HID ** -0.5, 0.1875),
    }


score_cap = 30.0
norm_eps = 1e-06

def direction_steps(chosen):
    cell_index = chosen + (chosen >= 12).astype(jnp.int32)
    return (cell_index // 5 - 2, cell_index % 5 - 2)

def attend(queries, keys_values, key_count, attention_out):
    group_size, block_len, row_width = queries.shape
    key_blocks = keys_values.shape[1]
    head_size = row_width // HEADS
    query_heads = queries.astype(jnp.float32).reshape(group_size, block_len, HEADS, head_size)
    key_heads = keys_values[..., :row_width].astype(jnp.float32).reshape(group_size, key_blocks * block_len, HEADS, head_size)
    value_heads = keys_values[..., row_width:].astype(jnp.float32).reshape(group_size, key_blocks * block_len, HEADS, head_size)
    raw_scores = jnp.einsum('cqhd,ckhd->chqk', query_heads, key_heads) * (1.0 / math.sqrt(head_size))
    capped = score_cap * jnp.tanh(raw_scores / score_cap)
    slot_index = jnp.arange(block_len, dtype=jnp.int32)
    live_keys = (slot_index[None, None, :] < key_count[:, :, None]).reshape(group_size, 1, 1, key_blocks * block_len)
    exp_scores = jnp.where(live_keys, jnp.exp(capped), jnp.zeros_like(capped))
    weights = (exp_scores / lax.optimization_barrier(jnp.sum(exp_scores, axis=-1, keepdims=True))).astype(jnp.bfloat16)
    context = jnp.einsum('chqk,ckhd->cqhd', weights.astype(jnp.float32), value_heads).astype(jnp.bfloat16)
    mixed_rows = jnp.dot(context.reshape(group_size * block_len, row_width), attention_out, preferred_element_type=jnp.float32)
    inv_norm = lax.rsqrt(lax.optimization_barrier(jnp.mean(mixed_rows * mixed_rows, axis=-1, keepdims=True)) + norm_eps)
    return (mixed_rows * inv_norm).astype(jnp.bfloat16).reshape(group_size, block_len, row_width)

def policy(rows, policy_in, policy_mid, policy_out):
    hidden = jax.nn.silu(jnp.dot(rows, policy_in, preferred_element_type=jnp.float32)).astype(jnp.bfloat16)
    for level_index in range(policy_mid.shape[0]):
        hidden = jax.nn.silu(jnp.dot(hidden, policy_mid[level_index], preferred_element_type=jnp.float32)).astype(jnp.bfloat16)
    return jnp.dot(hidden, policy_out, preferred_element_type=jnp.float32).astype(jnp.bfloat16)

def reference(agents, block_fill, neighbours, target_slot, attention_in, attention_out, policy_in, policy_mid, policy_out):
    rows_x, rows_y, block_len, row_width = agents.shape
    projected = jnp.dot(agents.reshape(-1, row_width), attention_in, preferred_element_type=jnp.float32).astype(jnp.bfloat16)
    projected = projected.reshape(rows_x, rows_y, block_len, 3 * row_width)
    padded = jnp.pad(projected[..., row_width:], ((2, 2), (2, 2), (0, 0), (0, 0)))
    padded_fill = jnp.pad(block_fill, 2)
    columns = jnp.arange(rows_y, dtype=jnp.int32)

    def one_row(block_row):
        step_x, step_y = direction_steps(neighbours[block_row])
        home_x = jnp.zeros((rows_y, 1), jnp.int32) + block_row + 2
        home_y = columns[:, None] + 2
        near_x = jnp.concatenate([home_x, home_x + step_x], axis=1)
        near_y = jnp.concatenate([home_y, home_y + step_y], axis=1)
        keys_values = padded[near_x, near_y]
        key_count = padded_fill[near_x, near_y]
        return attend(projected[block_row, :, :, :row_width], keys_values, key_count, attention_out)
    summary = lax.map(one_row, jnp.arange(rows_x, dtype=jnp.int32))
    observed = jnp.concatenate([agents, summary], axis=-1)
    live_slots = target_slot >= 0
    owner_index = jnp.where(live_slots, target_slot // BATCH, N_GX)
    batch_place = target_slot % BATCH
    tile_row = jnp.broadcast_to((columns // BY)[None, :, None], target_slot.shape)
    batch_obs = jnp.zeros((N_GX, N_GY, BATCH, 2 * row_width), jnp.bfloat16)
    batch_obs = batch_obs.at[owner_index, tile_row, batch_place].set(observed, mode='drop')
    batch_act = policy(batch_obs.reshape(-1, 2 * row_width), policy_in, policy_mid, policy_out)
    batch_act = batch_act.reshape(N_GX, N_GY, BATCH, -1)
    gathered = batch_act[jnp.where(live_slots, owner_index, 0), tile_row, batch_place]
    actions = jnp.where(live_slots[..., None], gathered, jnp.zeros_like(gathered))
    return (actions, batch_obs)
```

```python
import functools
import math

import jax
import jax.numpy as jnp
from jax import lax
from jax.experimental import pallas as pl
from jax.experimental.pallas import tpu as pltpu
from jax.sharding import PartitionSpec as P

HEADS = 4
LIVE = 96
REACH = 2
SCORE_CAP = 30.0
NORM_EPS = 1e-06
MIB = 1 << 20
BF16 = jnp.bfloat16
F32 = jnp.float32


def nt_dot(a, b):
    return lax.dot_general(a, b, (((1,), (1,)), ((), ())), preferred_element_type=F32)


def key_tables(fill_ref, near_ref, lx, ly, blocks_x, blocks_y, row_x, row_y):
    rows_x, rows_y = fill_ref.shape
    columns = blocks_y + 2 * REACH
    home_x = row_x * blocks_x + lx
    home_y = row_y * blocks_y + ly
    where_to = [lx * columns + ly + REACH]
    counts = [fill_ref[home_x, home_y]]
    for d in range(near_ref.shape[2]):
        direction = near_ref[lx, ly, d]
        cell = direction + jnp.where(direction >= 12, 1, 0)
        cell_x = (cell * 13) >> 6
        step_x = cell_x - REACH
        step_y = cell - cell_x * 5 - REACH
        at_x = home_x + step_x
        at_y = home_y + step_y
        inside = (at_x >= 0) & (at_x < rows_x) & (at_y >= 0) & (at_y < rows_y)
        safe_x = jnp.clip(at_x, 0, rows_x - 1)
        safe_y = jnp.clip(at_y, 0, rows_y - 1)
        counts.append(jnp.where(inside, fill_ref[safe_x, safe_y], 0))
        tile_x = jnp.where(safe_x >= blocks_x, 1, 0)
        other = jnp.where(tile_x == row_x, 0, 1)
        in_x = safe_x - tile_x * blocks_x
        where_to.append((other * blocks_x + in_x) * columns + ly + step_y + REACH)
    return where_to, counts


def attention_kernel(
    fill_ref,
    near_ref,
    place_ref,
    target_ref,
    own_ref,
    other_ref,
    low_ref,
    high_ref,
    other_low_ref,
    other_high_ref,
    weight_in_ref,
    weight_out_ref,
    summary_ref,
    packed_ref,
    keys_ref,
    values_ref,
    padded_ref,
):
    blocks_x, blocks_y = own_ref.shape[:2]
    width = own_ref.shape[-1]
    head = width // HEADS
    columns = blocks_y + 2 * REACH
    row_x = place_ref[0]
    row_y = place_ref[1]
    capacity = packed_ref.shape[0]
    weight_kv = weight_in_ref[:, width:]
    weight_q = weight_in_ref[:, :width]
    sources = ((low_ref, own_ref, high_ref), (other_low_ref, other_ref, other_high_ref))
    for o in range(2):
        for x in range(blocks_x):
            first = (o * blocks_x + x) * columns
            for part in sources[o]:
                count = part.shape[1]
                rows = part[x].reshape(count * LIVE, width)
                both = jnp.dot(rows, weight_kv, preferred_element_type=F32).astype(BF16)
                both = both.reshape(count, LIVE, 2 * width)
                keys_ref[first : first + count] = both[:, :, :width]
                values_ref[first : first + count] = both[:, :, width:]
                first += count

    key_blocks = near_ref.shape[2] + 1
    lane = lax.broadcasted_iota(jnp.int32, (1, key_blocks * LIVE), 1)
    head_of = lax.broadcasted_iota(jnp.int32, (1, width), 1) // head
    padded_ref[...] = jnp.zeros_like(padded_ref)
    for lx in range(blocks_x):
        for ly in range(blocks_y):
            b = lx * blocks_y + ly
            where_to, counts = key_tables(
                fill_ref, near_ref, lx, ly, blocks_x, blocks_y, row_x, row_y
            )
            query = jnp.dot(own_ref[lx, ly], weight_q, preferred_element_type=F32).astype(BF16)
            split = jnp.concatenate(
                [jnp.where(head_of == h, query, jnp.zeros_like(query)) for h in range(HEADS)],
                axis=0,
            )
            keys = jnp.concatenate([keys_ref[i] for i in where_to], axis=0)
            values = jnp.concatenate([values_ref[i] for i in where_to], axis=0)
            end = jnp.full(lane.shape, counts[0], jnp.int32)
            for j in range(1, key_blocks):
                end = jnp.where(lane >= j * LIVE, counts[j] + j * LIVE, end)
            raw = nt_dot(split, keys)
            capped = jnp.tanh(raw * (1.0 / (math.sqrt(head) * SCORE_CAP)))
            weight = jnp.exp(capped * SCORE_CAP)
            weight = jnp.where(lane < end, weight, 0.0)
            total = jnp.sum(weight, axis=-1, keepdims=True)
            mixed = jnp.dot(weight.astype(BF16), values, preferred_element_type=F32)
            mixed = mixed * (1.0 / total)
            context = mixed[:LIVE]
            for h in range(1, HEADS):
                context = jnp.where(head_of == h, mixed[h * LIVE : (h + 1) * LIVE], context)
            out = jnp.dot(
                context.astype(BF16), weight_out_ref[...], preferred_element_type=F32
            )
            scale = lax.rsqrt(jnp.mean(out * out, axis=-1, keepdims=True) + NORM_EPS)
            out = (out * scale).astype(BF16)
            summary_ref[lx, ly] = out
            padded_ref[b, :LIVE] = out

    block_len = padded_ref.shape[1]
    base = ((1 - row_x) * 2 + row_x) * capacity
    row = lax.broadcasted_iota(jnp.int32, (capacity, block_len), 0) + base
    pick = jnp.concatenate(
        [
            jnp.where(row == target_ref[lx, ly : ly + 1, :], 1.0, 0.0).astype(BF16)
            for lx in range(blocks_x)
            for ly in range(blocks_y)
        ],
        axis=1,
    )
    flat = padded_ref[...].reshape(blocks_x * blocks_y * block_len, width)
    packed_ref[...] = jnp.dot(pick, flat, preferred_element_type=F32).astype(BF16)


def silu(v):
    half = 0.5 * v
    return half + half * jnp.tanh(half)


def policy_kernel(
    fill_ref,
    place_ref,
    target_ref,
    other_target_ref,
    own_ref,
    other_ref,
    summary_ref,
    policy_in_ref,
    policy_mid_ref,
    policy_out_ref,
    actions_ref,
    batch_ref,
    x_ref,
    h_ref,
    g_ref,
    own_pad_ref,
    other_pad_ref,
):
    blocks_x, blocks_y = own_ref.shape[:2]
    width = own_ref.shape[-1]
    slots = blocks_x * blocks_y * LIVE
    block_len = actions_ref.shape[2]
    row_x = place_ref[0]
    row_y = place_ref[1]
    capacity = batch_ref.shape[0] // 2
    own = own_ref[...].reshape(slots, width)
    x_ref[:, :width] = own
    x_ref[:, width:] = summary_ref[...].reshape(slots, width)
    chunk = 256
    hidden = policy_in_ref.shape[1]
    for n in range(0, hidden, chunk):
        v = jnp.dot(x_ref[...], policy_in_ref[:, n : n + chunk], preferred_element_type=F32)
        h_ref[:, n : n + chunk] = silu(v).astype(BF16)
    now, later = h_ref, g_ref
    for m in range(policy_mid_ref.shape[0]):
        for n in range(0, hidden, chunk):
            v = jnp.dot(
                now[...], policy_mid_ref[m, :, n : n + chunk], preferred_element_type=F32
            )
            later[:, n : n + chunk] = silu(v).astype(BF16)
        now, later = later, now
    acts = jnp.dot(now[...], policy_out_ref[...], preferred_element_type=F32)
    slot = lax.broadcasted_iota(jnp.int32, (LIVE, 1), 0)
    for lx in range(blocks_x):
        for ly in range(blocks_y):
            b = lx * blocks_y + ly
            fill = fill_ref[row_x * blocks_x + lx, row_y * blocks_y + ly]
            act = jnp.where(slot < fill, acts[b * LIVE : (b + 1) * LIVE], 0.0)
            actions_ref[lx, ly, :LIVE] = act.astype(BF16)
            actions_ref[lx, ly, LIVE:] = jnp.zeros(
                (block_len - LIVE, act.shape[1]), BF16
            )

    own_pad_ref[...] = jnp.zeros_like(own_pad_ref)
    other_pad_ref[...] = jnp.zeros_like(other_pad_ref)
    for lx in range(blocks_x):
        for ly in range(blocks_y):
            b = lx * blocks_y + ly
            own_pad_ref[b, :LIVE] = x_ref[b * LIVE : (b + 1) * LIVE]
            other_pad_ref[b, :LIVE] = other_ref[lx, ly]
    count = blocks_x * blocks_y * block_len

    def picked(which_ref, source, rows):
        base = (row_x * 2 + source) * capacity
        row = lax.broadcasted_iota(jnp.int32, (capacity, block_len), 0) + base
        pick = jnp.concatenate(
            [
                jnp.where(row == which_ref[lx, ly : ly + 1, :], 1.0, 0.0).astype(BF16)
                for lx in range(blocks_x)
                for ly in range(blocks_y)
            ],
            axis=1,
        )
        return jnp.dot(pick, rows, preferred_element_type=F32).astype(BF16)

    mine = pl.ds(pl.multiple_of(row_x * capacity, capacity), capacity)
    theirs = pl.ds(pl.multiple_of((1 - row_x) * capacity, capacity), capacity)
    batch_ref[mine, :] = picked(target_ref, row_x, own_pad_ref[...].reshape(count, 2 * width))
    batch_ref[theirs, :width] = picked(
        other_target_ref, 1 - row_x, other_pad_ref[...].reshape(count, width)
    )
    batch_ref[theirs, width:] = jnp.zeros((capacity, width), BF16)


VMEM = pl.BlockSpec(memory_space=pltpu.VMEM)
SMEM = pl.BlockSpec(memory_space=pltpu.SMEM)


def on_device(
    agents,
    block_fill,
    neighbours,
    target_slot,
    attention_in,
    attention_out,
    policy_in,
    policy_mid,
    policy_out,
):
    blocks_x, blocks_y, block_len, width = agents.shape
    all_blocks = blocks_x * blocks_y
    owners = lax.axis_size("gx")
    count_y = lax.axis_size("gy")
    row_x = lax.axis_index("gx")
    capacity = 3 * all_blocks * block_len // (4 * owners)
    hidden = policy_in.shape[1]
    acts = policy_out.shape[1]
    place = jnp.stack([row_x, lax.axis_index("gy")]).astype(jnp.int32)

    swap = [(0, 1), (1, 0)]
    up = [(i, i + 1) for i in range(count_y - 1)]
    down = [(b, a) for a, b in up]
    own = agents[:, :, :LIVE]
    other = lax.ppermute(own, "gx", swap)
    low = lax.ppermute(own[:, blocks_y - REACH :], "gy", up)
    high = lax.ppermute(own[:, :REACH], "gy", down)
    other_low = lax.ppermute(other[:, blocks_y - REACH :], "gy", up)
    other_high = lax.ppermute(other[:, :REACH], "gy", down)
    other_target = lax.ppermute(target_slot, "gx", swap)

    window = blocks_x * owners * (blocks_y + 2 * REACH)
    summary, packed = pl.pallas_call(
        attention_kernel,
        out_shape=(
            jax.ShapeDtypeStruct((blocks_x, blocks_y, LIVE, width), BF16),
            jax.ShapeDtypeStruct((capacity, width), BF16),
        ),
        in_specs=[SMEM, SMEM, SMEM] + [VMEM] * 9,
        out_specs=(VMEM, VMEM),
        scratch_shapes=[
            pltpu.VMEM((window, LIVE, width), BF16),
            pltpu.VMEM((window, LIVE, width), BF16),
            pltpu.VMEM((all_blocks, block_len, width), BF16),
        ],
        compiler_params=pltpu.CompilerParams(vmem_limit_bytes=32 * MIB),
        name="attention",
    )(
        block_fill,
        neighbours,
        place,
        target_slot,
        own,
        other,
        low,
        high,
        other_low,
        other_high,
        attention_in,
        attention_out,
    )
    arrived = lax.ppermute(packed, "gx", swap)
    slots = all_blocks * LIVE
    rows = owners * capacity
    actions, batch = pl.pallas_call(
        policy_kernel,
        out_shape=(
            jax.ShapeDtypeStruct((blocks_x, blocks_y, block_len, acts), BF16),
            jax.ShapeDtypeStruct((rows, 2 * width), BF16),
        ),
        in_specs=[SMEM, SMEM] + [VMEM] * 8,
        out_specs=(VMEM, VMEM),
        scratch_shapes=[
            pltpu.VMEM((slots, 2 * width), BF16),
            pltpu.VMEM((slots, hidden), BF16),
            pltpu.VMEM((slots, hidden), BF16),
            pltpu.VMEM((all_blocks, block_len, 2 * width), BF16),
            pltpu.VMEM((all_blocks, block_len, width), BF16),
        ],
        compiler_params=pltpu.CompilerParams(vmem_limit_bytes=40 * MIB),
        cost_estimate=pl.CostEstimate(
            flops=2 * slots * hidden * (2 * width + 2 * hidden + acts),
            bytes_accessed=12 * MIB,
            transcendentals=3 * slots * hidden,
        ),
        name="policy",
    )(
        block_fill,
        place,
        target_slot,
        other_target,
        own,
        other,
        summary,
        policy_in,
        policy_mid,
        policy_out,
    )
    batch = lax.dynamic_update_slice(batch, arrived, ((1 - row_x) * capacity, width))
    return actions, batch.reshape(1, 1, rows, 2 * width)


def solution(mesh):
    return jax.shard_map(
        on_device,
        mesh=mesh,
        in_specs=(
            P("gx", "gy", None, None),
            P(),
            P("gx", "gy", None),
            P("gx", "gy", None),
            P(),
            P(),
            P(),
            P(),
            P(),
        ),
        out_specs=(P("gx", "gy", None, None), P("gx", "gy", None, None)),
        check_vma=False,
    )
```

```python
import math

import jax
import jax.numpy as jnp
from jax import lax
from jax.experimental import pallas as pl
from jax.experimental.pallas import tpu as pltpu
from jax.sharding import PartitionSpec as P

HEADS = 4
LIVE = 96
REACH = 2
SCORE_CAP = 30.0
NORM_EPS = 1e-06
LOG2_E = math.log2(math.e)
TARGET_ROWS = 8
MIB = 1 << 20
BF16 = jnp.bfloat16
F32 = jnp.float32


def nt_dot(a, b):
    return lax.dot_general(a, b, (((1,), (1,)), ((), ())), preferred_element_type=F32)


def key_tables(fill_ref, near_ref, lx, ly, columns, first, place):
    row_x, row_y, blocks_x, blocks_y = place
    rows_x, rows_y = fill_ref.shape
    home_x = row_x * blocks_x + lx
    home_y = row_y * blocks_y + ly
    where_to = [lx * columns + ly - first + REACH]
    counts = [fill_ref[home_x, home_y]]
    for d in range(near_ref.shape[2]):
        direction = near_ref[lx, ly, d]
        cell = direction + jnp.where(direction >= 12, 1, 0)
        cell_x = (cell * 13) >> 6
        step_x = cell_x - REACH
        step_y = cell - cell_x * 5 - REACH
        at_x = home_x + step_x
        at_y = home_y + step_y
        inside = (at_x >= 0) & (at_x < rows_x) & (at_y >= 0) & (at_y < rows_y)
        safe_x = jnp.clip(at_x, 0, rows_x - 1)
        safe_y = jnp.clip(at_y, 0, rows_y - 1)
        counts.append(jnp.where(inside, fill_ref[safe_x, safe_y], 0))
        tile_x = jnp.where(safe_x >= blocks_x, 1, 0)
        other = jnp.where(tile_x == row_x, 0, 1)
        in_x = safe_x - tile_x * blocks_x
        where_to.append((other * blocks_x + in_x) * columns + ly - first + step_y + REACH)
    return where_to, counts


def one_hot(base, capacity, block_len, target_rows):
    row = lax.broadcasted_iota(jnp.int32, (capacity, block_len), 0) + base
    row = row.astype(F32)
    return jnp.concatenate(
        [jnp.where(row == target, 1.0, 0.0).astype(BF16) for target in target_rows], axis=1
    )


def place(pick, pad_ref):
    blocks, block_len, width = pad_ref.shape
    flat = pad_ref[...].reshape(blocks * block_len, width)
    return jnp.dot(pick, flat, preferred_element_type=F32)


def sent_targets(ref, first, count):
    start = ref.shape[0] - TARGET_ROWS
    half = ref.shape[1] // 2
    both = ref[start : start + TARGET_ROWS].astype(F32)
    rows = both[:, :half] * 256.0 + both[:, half:]
    return [rows[b : b + 1] for b in range(first, first + count)]


def spread(pad_ref, first, rows, blocks):
    _, block_len, width = pad_ref.shape
    for b in range(blocks):
        pad_ref[first + b, :LIVE] = rows[b * LIVE : (b + 1) * LIVE]
        pad_ref[first + b, LIVE:] = jnp.zeros((block_len - LIVE, width), pad_ref.dtype)


def stage_kernel(place_ref, target_hbm, agents_hbm, off_ref, inn_ref, target_ref, sems):
    blocks_x, _, _, _ = agents_hbm.shape
    core = place_ref[1] & 1
    rows = REACH * LIVE
    targets = pltpu.make_async_copy(target_hbm, target_ref, sems.at[2, 0])
    targets.start()
    copies = []
    for x in range(blocks_x):
        for ref, column, s in ((off_ref, core * REACH, 0), (inn_ref, REACH - core * REACH, 1)):
            for c in range(REACH):
                copies.append(
                    pltpu.make_async_copy(
                        agents_hbm.at[x, column + c, pl.ds(0, LIVE)],
                        ref.at[pl.ds(x * rows + c * LIVE, LIVE)],
                        sems.at[s, x * REACH + c],
                    )
                )
    for copy in copies:
        copy.start()
    targets.wait()
    halves = []
    for column in (core * REACH, REACH - core * REACH):
        for x in range(blocks_x):
            for c in range(REACH):
                halves.append(target_ref[x, pl.ds(column + c, 1), :])
    target = jnp.concatenate(halves, axis=0)
    high = target >> 8
    low = target - high * 256
    split = jnp.concatenate([high, low], axis=1).astype(F32).astype(BF16)
    inn_ref[blocks_x * rows :] = split
    for copy in copies:
        copy.wait()


def local_kernel(
    place_ref,
    off_ref,
    inn_ref,
    weight_in_hbm,
    weight_out_hbm,
    weight_in_ref,
    weight_out_ref,
    own_rows_ref,
    pad_ref,
    sems,
):
    copies = [
        pltpu.make_async_copy(weight_in_hbm, weight_in_ref, sems.at[0]),
        pltpu.make_async_copy(weight_out_hbm, weight_out_ref, sems.at[1]),
    ]
    for copy in copies:
        copy.start()
    capacity = own_rows_ref.shape[0]
    blocks, block_len, _ = pad_ref.shape
    row_x = place_ref[0]
    spread(pad_ref, 0, off_ref, blocks // 2)
    spread(pad_ref, blocks // 2, inn_ref, blocks // 2)
    pick = one_hot(
        (row_x * 2 + row_x) * capacity, capacity, block_len, sent_targets(inn_ref, 0, blocks)
    )
    own_rows_ref[...] = place(pick, pad_ref).astype(BF16)
    for copy in copies:
        copy.wait()


def attend(home_ref, first, sources, fill_ref, near_ref, place_ref, weights, window):
    weight_in_ref, weight_out_ref = weights
    keys_ref, values_ref, context_ref = window
    width = weight_out_ref.shape[0]
    head = width // HEADS
    half_rows = context_ref.shape[0]
    blocks_x = half_rows // (REACH * LIVE)
    blocks_y = 2 * REACH
    columns = 3 * REACH
    row_x = place_ref[0]
    row_y = place_ref[1]
    for o, column, ref in sources:
        rows = ref[:half_rows]
        both = jnp.dot(rows, weight_in_ref[:, width:], preferred_element_type=F32).astype(BF16)
        both = both.reshape(blocks_x * REACH, LIVE, 2 * width)
        for x in range(blocks_x):
            at = (o * blocks_x + x) * columns + column
            keys_ref[pl.ds(at, REACH)] = both[x * REACH : (x + 1) * REACH, :, :width]
            values_ref[pl.ds(at, REACH)] = both[x * REACH : (x + 1) * REACH, :, width:]

    key_blocks = near_ref.shape[2] + 1
    lane = lax.broadcasted_iota(jnp.int32, (1, key_blocks * LIVE), 1)
    head_of = lax.broadcasted_iota(jnp.int32, (1, width), 1) // head
    queries = jnp.dot(
        home_ref[:half_rows], weight_in_ref[:, :width], preferred_element_type=F32
    ).astype(BF16)
    for i in range(blocks_x * REACH):
        lx = i // REACH
        ly = first + i % REACH
        where_to, counts = key_tables(
            fill_ref, near_ref, lx, ly, columns, first, (row_x, row_y, blocks_x, blocks_y)
        )
        query = queries[i * LIVE : (i + 1) * LIVE]
        split = jnp.concatenate(
            [jnp.where(head_of == h, query, jnp.zeros_like(query)) for h in range(HEADS)],
            axis=0,
        )
        keys = jnp.concatenate([keys_ref[w] for w in where_to], axis=0)
        values = jnp.concatenate([values_ref[w] for w in where_to], axis=0)
        end = jnp.full(lane.shape, counts[0], jnp.int32)
        for j in range(1, key_blocks):
            end = jnp.where(lane >= j * LIVE, counts[j] + j * LIVE, end)
        raw = nt_dot(split, keys)
        capped = jnp.tanh(raw * (1.0 / (math.sqrt(head) * SCORE_CAP)))
        weight = jnp.exp2(capped * (SCORE_CAP * LOG2_E))
        weight = jnp.where(lane < end, weight, 0.0)
        total = jnp.sum(weight, axis=-1, keepdims=True)
        weight = (weight * (1.0 / total)).astype(BF16)
        mixed = jnp.dot(weight, values, preferred_element_type=F32)
        context = mixed[:LIVE]
        for h in range(1, HEADS):
            context = jnp.where(head_of == h, mixed[h * LIVE : (h + 1) * LIVE], context)
        context_ref[i * LIVE : (i + 1) * LIVE] = context.astype(BF16)
    out = jnp.dot(context_ref[...], weight_out_ref[...], preferred_element_type=F32)
    scale = lax.rsqrt(jnp.mean(out * out, axis=-1, keepdims=True) + NORM_EPS)
    return (out * scale).astype(BF16)


def inner_kernel(
    fill_ref,
    near_ref,
    place_ref,
    off_ref,
    inn_ref,
    other_off_ref,
    other_inn_ref,
    side_ref,
    other_side_ref,
    weight_in_ref,
    weight_out_ref,
    policy_in_hbm,
    policy_mid_hbm,
    policy_out_hbm,
    summary_ref,
    packed_ref,
    own_ref,
    other_rows_ref,
    policy_in_ref,
    policy_mid_ref,
    policy_out_ref,
    keys_ref,
    values_ref,
    context_ref,
    pad_ref,
    sems,
):
    pairs = (
        (policy_in_hbm, policy_in_ref),
        (policy_mid_hbm, policy_mid_ref),
        (policy_out_hbm, policy_out_ref),
    )
    copies = [pltpu.make_async_copy(a, b, sems.at[i]) for i, (a, b) in enumerate(pairs)]
    for copy in copies:
        copy.start()
    row_x = place_ref[0]
    core = place_ref[1] & 1
    at_inn = REACH
    at_off = 2 * REACH * core
    at_side = 2 * REACH - 2 * REACH * core
    sources = (
        (0, at_off, off_ref),
        (0, at_inn, inn_ref),
        (1, at_off, other_off_ref),
        (1, at_inn, other_inn_ref),
        (0, at_side, side_ref),
        (1, at_side, other_side_ref),
    )
    out = attend(
        inn_ref,
        REACH - core * REACH,
        sources,
        fill_ref,
        near_ref,
        place_ref,
        (weight_in_ref, weight_out_ref),
        (keys_ref, values_ref, context_ref),
    )
    summary_ref[...] = out
    capacity = packed_ref.shape[0]
    blocks, block_len, _ = pad_ref.shape
    each = blocks // 2
    spread(pad_ref, 0, out, each)
    rows = sent_targets(inn_ref, each, each)
    for ref, owner in ((packed_ref, 1 - row_x), (own_ref, row_x)):
        pick = one_hot((owner * 2 + row_x) * capacity, capacity, block_len, rows)
        ref[...] = place(pick, pad_ref.at[:each]).astype(BF16)
    spread(pad_ref, 0, other_off_ref, each)
    spread(pad_ref, each, other_inn_ref, each)
    pick = one_hot(
        (row_x * 2 + 1 - row_x) * capacity,
        capacity,
        block_len,
        sent_targets(other_inn_ref, 0, blocks),
    )
    other_rows_ref[...] = place(pick, pad_ref).astype(BF16)
    for copy in copies:
        copy.wait()


def outer_kernel(
    fill_ref,
    near_ref,
    place_ref,
    off_ref,
    inn_ref,
    other_off_ref,
    other_inn_ref,
    side_ref,
    other_side_ref,
    weight_in_ref,
    weight_out_ref,
    inner_packed_ref,
    summary_ref,
    packed_ref,
    keys_ref,
    values_ref,
    context_ref,
    pad_ref,
):
    row_x = place_ref[0]
    core = place_ref[1] & 1
    at_off = REACH
    at_inn = 2 * REACH - 2 * REACH * core
    at_side = 2 * REACH * core
    sources = (
        (0, at_off, off_ref),
        (0, at_inn, inn_ref),
        (1, at_off, other_off_ref),
        (1, at_inn, other_inn_ref),
        (0, at_side, side_ref),
        (1, at_side, other_side_ref),
    )
    out = attend(
        off_ref,
        core * REACH,
        sources,
        fill_ref,
        near_ref,
        place_ref,
        (weight_in_ref, weight_out_ref),
        (keys_ref, values_ref, context_ref),
    )
    summary_ref[...] = out
    capacity = packed_ref.shape[0]
    each, block_len, _ = pad_ref.shape
    spread(pad_ref, 0, out, each)
    rows = sent_targets(inn_ref, 0, each)
    pick = one_hot(((1 - row_x) * 2 + row_x) * capacity, capacity, block_len, rows)
    packed_ref[...] = (place(pick, pad_ref) + inner_packed_ref[...].astype(F32)).astype(BF16)


def silu(v):
    half = 0.5 * v
    return half + half * jnp.tanh(half)


def policy_kernel(
    fill_ref,
    place_ref,
    off_ref,
    inn_ref,
    off_summary_ref,
    inn_summary_ref,
    own_rows_ref,
    own_inner_ref,
    other_rows_ref,
    policy_in_ref,
    policy_mid_ref,
    policy_out_ref,
    actions_ref,
    batch_ref,
    x_ref,
    h_ref,
    g_ref,
    pad_ref,
):
    width = off_ref.shape[1]
    blocks_x, blocks_y, block_len, _ = actions_ref.shape
    row_x = place_ref[0]
    row_y = place_ref[1]
    core = row_y & 1
    capacity = batch_ref.shape[0] // 2
    half_rows = off_ref.shape[0]
    x_ref[:half_rows, :width] = off_ref[...]
    x_ref[half_rows:, :width] = inn_ref[:half_rows]
    x_ref[:half_rows, width:] = off_summary_ref[...]
    x_ref[half_rows:, width:] = inn_summary_ref[...]
    chunk = 256
    hidden = policy_in_ref.shape[1]
    for n in range(0, hidden, chunk):
        v = jnp.dot(x_ref[...], policy_in_ref[:, n : n + chunk], preferred_element_type=F32)
        h_ref[:, n : n + chunk] = silu(v).astype(BF16)
    now, later = h_ref, g_ref
    for m in range(policy_mid_ref.shape[0]):
        for n in range(0, hidden, chunk):
            v = jnp.dot(
                now[...], policy_mid_ref[m, :, n : n + chunk], preferred_element_type=F32
            )
            later[:, n : n + chunk] = silu(v).astype(BF16)
        now, later = later, now
    acts = jnp.dot(now[...], policy_out_ref[...], preferred_element_type=F32)
    slot = lax.broadcasted_iota(jnp.int32, (LIVE, 1), 0)
    for half, first in enumerate((core * REACH, REACH - core * REACH)):
        for i in range(blocks_x * REACH):
            lx = i // REACH
            ly = first + i % REACH
            b = half * blocks_x * REACH + i
            fill = fill_ref[row_x * blocks_x + lx, row_y * blocks_y + ly]
            act = jnp.where(slot < fill, acts[b * LIVE : (b + 1) * LIVE], 0.0)
            actions_ref[lx, ly, :LIVE] = act.astype(BF16)
            actions_ref[lx, ly, LIVE:] = jnp.zeros((block_len - LIVE, act.shape[1]), BF16)

    mine = pl.ds(pl.multiple_of(row_x * capacity, capacity), capacity)
    theirs = pl.ds(pl.multiple_of((1 - row_x) * capacity, capacity), capacity)
    each = pad_ref.shape[0]
    spread(pad_ref, 0, off_summary_ref, each)
    rows = sent_targets(inn_ref, 0, each)
    pick = one_hot((row_x * 2 + row_x) * capacity, capacity, block_len, rows)
    batch_ref[mine, :width] = own_rows_ref[...]
    batch_ref[mine, width:] = (place(pick, pad_ref) + own_inner_ref[...].astype(F32)).astype(BF16)
    batch_ref[theirs, :width] = other_rows_ref[...]
    batch_ref[theirs, width:] = jnp.zeros((capacity, width), BF16)


VMEM = pl.BlockSpec(memory_space=pltpu.VMEM)
SMEM = pl.BlockSpec(memory_space=pltpu.SMEM)
HBM = pl.BlockSpec(memory_space=pltpu.HBM)
SDS = jax.ShapeDtypeStruct


def in_hbm(*arrays):
    return tuple(pltpu.with_memory_space_constraint(a, pltpu.HBM) for a in arrays)


def on_device(
    agents,
    block_fill,
    neighbours,
    target_slot,
    attention_in,
    attention_out,
    policy_in,
    policy_mid,
    policy_out,
):
    blocks_x, blocks_y, block_len, width = agents.shape
    all_blocks = blocks_x * blocks_y
    owners = lax.axis_size("gx")
    count_y = lax.axis_size("gy")
    row_x = lax.axis_index("gx")
    capacity = 3 * all_blocks * block_len // (4 * owners)
    hidden = policy_in.shape[1]
    acts = policy_out.shape[1]
    slots = all_blocks * LIVE
    half_rows = slots // 2
    rows = owners * capacity
    where = jnp.stack([row_x, lax.axis_index("gy")]).astype(jnp.int32)

    swap = [(0, 1), (1, 0)]
    across = [(i, i - 1) for i in range(2, count_y, 2)]
    across += [(i, i + 1) for i in range(1, count_y - 1, 2)]
    beside = [(i, i ^ 1) for i in range(count_y)]
    diagonal = [
        (g * count_y + a, (1 - g) * count_y + b) for g in range(owners) for a, b in across
    ]

    off, inn = pl.pallas_call(
        stage_kernel,
        out_shape=(SDS((half_rows, width), BF16), SDS((half_rows + TARGET_ROWS, width), BF16)),
        in_specs=[SMEM, HBM, HBM],
        out_specs=(VMEM, VMEM),
        scratch_shapes=[
            pltpu.VMEM((blocks_x, blocks_y, block_len), jnp.int32),
            pltpu.SemaphoreType.DMA((3, all_blocks // 2)),
        ],
        compiler_params=pltpu.CompilerParams(vmem_limit_bytes=4 * MIB),
        name="stage",
    )(where, *in_hbm(target_slot, agents))
    other_inn = lax.ppermute(inn, "gx", swap)
    other_off = lax.ppermute(off, "gx", swap)
    side_off = lax.ppermute(off, "gy", across)
    side_inn = lax.ppermute(inn, "gy", beside)
    attention_in, attention_out, own_rows = pl.pallas_call(
        local_kernel,
        out_shape=(
            SDS(attention_in.shape, BF16),
            SDS(attention_out.shape, BF16),
            SDS((capacity, width), BF16),
        ),
        in_specs=[SMEM, VMEM, VMEM, HBM, HBM],
        out_specs=(VMEM,) * 3,
        scratch_shapes=[
            pltpu.VMEM((all_blocks, block_len, width), BF16),
            pltpu.SemaphoreType.DMA((2,)),
        ],
        compiler_params=pltpu.CompilerParams(vmem_limit_bytes=8 * MIB),
        cost_estimate=pl.CostEstimate(
            flops=2 * capacity * all_blocks * block_len * width,
            bytes_accessed=8 * MIB,
            transcendentals=0,
        ),
        name="local",
    )(where, off, inn, *in_hbm(attention_in, attention_out))
    own_rows, other_inn, off_late = lax.optimization_barrier((own_rows, other_inn, off))
    other_side_off = lax.ppermute(off_late, ("gx", "gy"), diagonal)
    other_side_inn = lax.ppermute(other_inn, "gy", beside)

    window = blocks_x * owners * 3 * REACH
    scratch = [
        pltpu.VMEM((window, LIVE, width), BF16),
        pltpu.VMEM((window, LIVE, width), BF16),
        pltpu.VMEM((half_rows, width), BF16),
    ]
    scores = all_blocks // 2 * HEADS * LIVE * 5 * LIVE
    cost = pl.CostEstimate(
        flops=2 * (2 * scores + window * LIVE * 2 * width) * width,
        bytes_accessed=8 * MIB,
        transcendentals=2 * scores,
    )
    inn_summary, packed, own_inner, other_rows, policy_in, policy_mid, policy_out = pl.pallas_call(
        inner_kernel,
        out_shape=(
            SDS((half_rows, width), BF16),
            SDS((capacity, width), BF16),
            SDS((capacity, width), BF16),
            SDS((capacity, width), BF16),
            SDS(policy_in.shape, BF16),
            SDS(policy_mid.shape, BF16),
            SDS(policy_out.shape, BF16),
        ),
        in_specs=[SMEM] * 3 + [VMEM] * 8 + [HBM] * 3,
        out_specs=(VMEM,) * 7,
        scratch_shapes=scratch
        + [
            pltpu.VMEM((all_blocks, block_len, width), BF16),
            pltpu.SemaphoreType.DMA((3,)),
        ],
        compiler_params=pltpu.CompilerParams(vmem_limit_bytes=14 * MIB),
        cost_estimate=cost,
        name="inner",
    )(
        block_fill,
        neighbours,
        where,
        off,
        inn,
        other_off,
        other_inn,
        side_inn,
        other_side_inn,
        attention_in,
        attention_out,
        *in_hbm(policy_in, policy_mid, policy_out),
    )
    off_summary, packed = pl.pallas_call(
        outer_kernel,
        out_shape=(SDS((half_rows, width), BF16), SDS((capacity, width), BF16)),
        in_specs=[SMEM] * 3 + [VMEM] * 9,
        out_specs=(VMEM, VMEM),
        scratch_shapes=scratch + [pltpu.VMEM((all_blocks // 2, block_len, width), BF16)],
        compiler_params=pltpu.CompilerParams(vmem_limit_bytes=14 * MIB),
        cost_estimate=cost,
        name="outer",
    )(
        block_fill,
        neighbours,
        where,
        off,
        inn,
        other_off,
        other_inn,
        side_off,
        other_side_off,
        attention_in,
        attention_out,
        packed,
    )
    arrived = lax.ppermute(packed, "gx", swap)
    actions, batch = pl.pallas_call(
        policy_kernel,
        out_shape=(
            SDS((blocks_x, blocks_y, block_len, acts), BF16),
            SDS((rows, 2 * width), BF16),
        ),
        in_specs=[SMEM] * 2 + [VMEM] * 10,
        out_specs=(VMEM, VMEM),
        scratch_shapes=[
            pltpu.VMEM((slots, 2 * width), BF16),
            pltpu.VMEM((slots, hidden), BF16),
            pltpu.VMEM((slots, hidden), BF16),
            pltpu.VMEM((all_blocks // 2, block_len, width), BF16),
        ],
        compiler_params=pltpu.CompilerParams(vmem_limit_bytes=16 * MIB),
        cost_estimate=pl.CostEstimate(
            flops=2 * slots * hidden * (2 * width + 2 * hidden + acts),
            bytes_accessed=12 * MIB,
            transcendentals=3 * slots * hidden,
        ),
        name="policy",
    )(
        block_fill,
        where,
        off,
        inn,
        off_summary,
        inn_summary,
        own_rows,
        own_inner,
        other_rows,
        policy_in,
        policy_mid,
        policy_out,
    )
    batch = lax.dynamic_update_slice(batch, arrived, ((1 - row_x) * capacity, width))
    return actions, batch.reshape(1, 1, rows, 2 * width)


def solution(mesh):
    return jax.shard_map(
        on_device,
        mesh=mesh,
        in_specs=(
            P("gx", "gy", None, None),
            P(),
            P("gx", "gy", None),
            P("gx", "gy", None),
            P(),
            P(),
            P(),
            P(),
            P(),
        ),
        out_specs=(P("gx", "gy", None, None), P("gx", "gy", None, None)),
        check_vma=False,
    )
```

```python
import math

import jax
import jax.numpy as jnp
from jax import lax
from jax.experimental import pallas as pl
from jax.experimental.pallas import tpu as pltpu
from jax.sharding import PartitionSpec as P

HEADS = 4
LIVE = 96
REACH = 2
SCORE_CAP = 30.0
NORM_EPS = 1e-06
LOG2_E = math.log2(math.e)
TARGET_ROWS = 8
MIB = 1 << 20
BF16 = jnp.bfloat16
F32 = jnp.float32


def nt_dot(a, b):
    return lax.dot_general(a, b, (((1,), (1,)), ((), ())), preferred_element_type=F32)


def key_tables(table_ref, fill_ref, near_ref, b, lx, ly, place):
    row_x, row_y, blocks_x, blocks_y = place
    rows_x, rows_y = fill_ref.shape
    columns = blocks_y + 2 * REACH
    key_blocks = near_ref.shape[2] + 1
    home_x = row_x * blocks_x + lx
    home_y = row_y * blocks_y + ly
    table_ref[b, 0] = lx * columns + ly + REACH
    table_ref[b, key_blocks] = fill_ref[home_x, home_y]
    for d in range(key_blocks - 1):
        direction = near_ref[lx, ly, d]
        cell = direction + jnp.where(direction >= 12, 1, 0)
        cell_x = (cell * 13) >> 6
        step_x = cell_x - REACH
        step_y = cell - cell_x * 5 - REACH
        at_x = home_x + step_x
        at_y = home_y + step_y
        inside = (at_x >= 0) & (at_x < rows_x) & (at_y >= 0) & (at_y < rows_y)
        safe_x = jnp.clip(at_x, 0, rows_x - 1)
        safe_y = jnp.clip(at_y, 0, rows_y - 1)
        tile_x = jnp.where(safe_x >= blocks_x, 1, 0)
        other = jnp.where(tile_x == row_x, 0, 1)
        in_x = safe_x - tile_x * blocks_x
        table_ref[b, 1 + d] = (other * blocks_x + in_x) * columns + ly + step_y + REACH
        table_ref[b, key_blocks + 1 + d] = jnp.where(inside, fill_ref[safe_x, safe_y], 0)


def one_hot(base, capacity, block_len, target_rows):
    row = lax.broadcasted_iota(jnp.int32, (capacity, block_len), 0) + base
    row = row.astype(F32)
    return jnp.concatenate(
        [jnp.where(row == target, 1.0, 0.0).astype(BF16) for target in target_rows], axis=1
    )


def place(pick, pad_ref):
    blocks, block_len, width = pad_ref.shape
    flat = pad_ref[...].reshape(blocks * block_len, width)
    return jnp.dot(pick, flat, preferred_element_type=F32)


def sent_targets(ref, first, count):
    start = ref.shape[0] - TARGET_ROWS
    half = ref.shape[1] // 2
    both = ref[start : start + TARGET_ROWS].astype(F32)
    rows = both[:, :half] * 256.0 + both[:, half:]
    return [rows[b : b + 1] for b in range(first, first + count)]


def spread(pad_ref, first, rows, blocks):
    _, block_len, width = pad_ref.shape
    for b in range(blocks):
        pad_ref[first + b, :LIVE] = rows[b * LIVE : (b + 1) * LIVE]
        pad_ref[first + b, LIVE:] = jnp.zeros((block_len - LIVE, width), pad_ref.dtype)


def stage_kernel(place_ref, target_hbm, agents_hbm, off_ref, inn_ref, target_ref, sems):
    blocks_x, _, _, _ = agents_hbm.shape
    core = place_ref[1] & 1
    rows = REACH * LIVE
    targets = pltpu.make_async_copy(target_hbm, target_ref, sems.at[2, 0])
    targets.start()
    copies = []
    for x in range(blocks_x):
        for ref, column, s in ((off_ref, core * REACH, 0), (inn_ref, REACH - core * REACH, 1)):
            copies.append(
                pltpu.make_async_copy(
                    agents_hbm.at[x, pl.ds(column, REACH), pl.ds(0, LIVE)],
                    ref.at[pl.ds(x * rows, rows)].reshape(REACH, LIVE, ref.shape[1]),
                    sems.at[s, x],
                )
            )
    for copy in copies:
        copy.start()
    targets.wait()
    halves = []
    for column in (core * REACH, REACH - core * REACH):
        for x in range(blocks_x):
            for c in range(REACH):
                halves.append(target_ref[x, pl.ds(column + c, 1), :])
    target = jnp.concatenate(halves, axis=0)
    high = target >> 8
    low = target - high * 256
    split = jnp.concatenate([high, low], axis=1).astype(F32).astype(BF16)
    inn_ref[blocks_x * rows :] = split
    for copy in copies:
        copy.wait()


def local_kernel(
    fill_ref,
    near_ref,
    place_ref,
    off_ref,
    inn_ref,
    weight_in_hbm,
    weight_out_hbm,
    weight_in_ref,
    weight_out_ref,
    own_rows_ref,
    pick_out_ref,
    table_ref,
    token_ref,
    pad_ref,
    sems,
):
    copies = [
        pltpu.make_async_copy(weight_in_hbm, weight_in_ref, sems.at[0]),
        pltpu.make_async_copy(weight_out_hbm, weight_out_ref, sems.at[1]),
    ]
    for copy in copies:
        copy.start()
    capacity = own_rows_ref.shape[0]
    blocks, block_len, _ = pad_ref.shape
    row_x = place_ref[0]
    core = place_ref[1] & 1
    place_of = (row_x, place_ref[1], blocks // (2 * REACH), 2 * REACH)
    for half, first in enumerate((core * REACH, REACH - core * REACH)):
        for i in range(blocks // 2):
            b = half * (blocks // 2) + i
            at = (i // REACH, first + i % REACH)
            key_tables(table_ref, fill_ref, near_ref, b, *at, place_of)
    spread(pad_ref, 0, off_ref, blocks // 2)
    spread(pad_ref, blocks // 2, inn_ref, blocks // 2)
    targets = sent_targets(inn_ref, 0, blocks)
    pick_out_ref[...] = one_hot(
        ((1 - row_x) * 2 + row_x) * capacity, capacity, block_len, targets
    )
    pick = one_hot((row_x * 2 + row_x) * capacity, capacity, block_len, targets)
    own_rows_ref[...] = place(pick, pad_ref).astype(BF16)
    token_ref[...] = jnp.zeros_like(token_ref)
    for copy in copies:
        copy.wait()


def attention_kernel(
    table_ref,
    place_ref,
    off_ref,
    inn_ref,
    other_off_ref,
    other_inn_ref,
    side_off_ref,
    side_inn_ref,
    other_side_off_ref,
    other_side_inn_ref,
    weight_in_ref,
    weight_out_ref,
    pick_out_ref,
    token_ref,
    summary_ref,
    packed_ref,
    keys_ref,
    values_ref,
    context_ref,
    pad_ref,
):
    width = weight_out_ref.shape[0]
    head = width // HEADS
    half_rows = off_ref.shape[0]
    each = half_rows // LIVE
    blocks_x = each // REACH
    columns = 4 * REACH
    core = place_ref[1] & 1
    at_off = REACH + REACH * core
    at_inn = 2 * REACH - REACH * core
    at_side_off = 3 * REACH * core
    at_side_inn = 3 * REACH - 3 * REACH * core
    sources = (
        (0, at_off, off_ref),
        (0, at_inn, inn_ref),
        (1, at_off, other_off_ref),
        (1, at_inn, other_inn_ref),
        (0, at_side_off, side_off_ref),
        (0, at_side_inn, side_inn_ref),
        (1, at_side_off, other_side_off_ref),
        (1, at_side_inn, other_side_inn_ref),
    )
    for o, column, ref in sources:
        rows = ref[:half_rows]
        both = jnp.dot(rows, weight_in_ref[:, width:], preferred_element_type=F32).astype(BF16)
        both = both.reshape(each, LIVE, 2 * width)
        for x in range(blocks_x):
            at = (o * blocks_x + x) * columns + column
            keys_ref[pl.ds(at, REACH)] = both[x * REACH : (x + 1) * REACH, :, :width]
            values_ref[pl.ds(at, REACH)] = both[x * REACH : (x + 1) * REACH, :, width:]

    key_blocks = table_ref.shape[1] // 2
    lane = lax.broadcasted_iota(jnp.int32, (1, key_blocks * LIVE), 1)
    head_of = lax.broadcasted_iota(jnp.int32, (1, width), 1) // head
    queries = [
        jnp.dot(ref[:half_rows], weight_in_ref[:, :width], preferred_element_type=F32).astype(BF16)
        for ref in (off_ref, inn_ref)
    ]
    for b in range(2 * each):
        where_to = [table_ref[b, j] for j in range(key_blocks)]
        counts = [table_ref[b, key_blocks + j] for j in range(key_blocks)]
        i = b % each
        query = queries[b // each][i * LIVE : (i + 1) * LIVE]
        split = jnp.concatenate(
            [jnp.where(head_of == h, query, jnp.zeros_like(query)) for h in range(HEADS)],
            axis=0,
        )
        keys = jnp.concatenate([keys_ref[w] for w in where_to], axis=0)
        values = jnp.concatenate([values_ref[w] for w in where_to], axis=0)
        end = jnp.full(lane.shape, counts[0], jnp.int32)
        for j in range(1, key_blocks):
            end = jnp.where(lane >= j * LIVE, counts[j] + j * LIVE, end)
        raw = nt_dot(split, keys)
        capped = jnp.tanh(raw * (1.0 / (math.sqrt(head) * SCORE_CAP)))
        weight = jnp.exp2(capped * (SCORE_CAP * LOG2_E))
        weight = jnp.where(lane < end, weight, 0.0)
        total = jnp.sum(weight, axis=-1, keepdims=True)
        weight = (weight * (1.0 / total)).astype(BF16)
        mixed = jnp.dot(weight, values, preferred_element_type=F32)
        context = mixed[:LIVE]
        for h in range(1, HEADS):
            context = jnp.where(head_of == h, mixed[h * LIVE : (h + 1) * LIVE], context)
        context_ref[b * LIVE : (b + 1) * LIVE] = context.astype(BF16)
    out = jnp.dot(context_ref[...], weight_out_ref[...], preferred_element_type=F32)
    scale = lax.rsqrt(jnp.mean(out * out, axis=-1, keepdims=True) + NORM_EPS)
    out = (out * scale).astype(BF16)
    summary_ref[...] = out
    spread(pad_ref, 0, out, 2 * each)
    packed_ref[...] = place(pick_out_ref[...], pad_ref).astype(BF16)


def silu(v):
    half = 0.5 * v
    return half + half * jnp.tanh(half)


def policy_kernel(
    table_ref,
    place_ref,
    off_ref,
    inn_ref,
    other_off_ref,
    other_inn_ref,
    summary_ref,
    own_rows_ref,
    policy_in_ref,
    policy_mid_ref,
    policy_out_ref,
    actions_ref,
    batch_ref,
    x_ref,
    h_ref,
    g_ref,
    pad_ref,
):
    width = off_ref.shape[1]
    blocks_x, blocks_y, block_len, _ = actions_ref.shape
    row_x = place_ref[0]
    core = place_ref[1] & 1
    capacity = batch_ref.shape[0] // 2
    half_rows = off_ref.shape[0]
    x_ref[:half_rows, :width] = off_ref[...]
    x_ref[half_rows:, :width] = inn_ref[:half_rows]
    x_ref[:, width:] = summary_ref[...]
    chunk = 256
    hidden = policy_in_ref.shape[1]
    for n in range(0, hidden, chunk):
        v = jnp.dot(x_ref[...], policy_in_ref[:, n : n + chunk], preferred_element_type=F32)
        h_ref[:, n : n + chunk] = silu(v).astype(BF16)
    now, later = h_ref, g_ref
    for m in range(policy_mid_ref.shape[0]):
        for n in range(0, hidden, chunk):
            v = jnp.dot(
                now[...], policy_mid_ref[m, :, n : n + chunk], preferred_element_type=F32
            )
            later[:, n : n + chunk] = silu(v).astype(BF16)
        now, later = later, now
    acts = jnp.dot(now[...], policy_out_ref[...], preferred_element_type=F32)
    slot = lax.broadcasted_iota(jnp.int32, (LIVE, 1), 0)
    for half, first in enumerate((core * REACH, REACH - core * REACH)):
        for i in range(blocks_x * REACH):
            lx = i // REACH
            ly = first + i % REACH
            b = half * blocks_x * REACH + i
            fill = table_ref[b, table_ref.shape[1] // 2]
            act = jnp.where(slot < fill, acts[b * LIVE : (b + 1) * LIVE], 0.0)
            actions_ref[lx, ly, :LIVE] = act.astype(BF16)
            actions_ref[lx, ly, LIVE:] = jnp.zeros((block_len - LIVE, act.shape[1]), BF16)

    mine = pl.ds(pl.multiple_of(row_x * capacity, capacity), capacity)
    theirs = pl.ds(pl.multiple_of((1 - row_x) * capacity, capacity), capacity)
    blocks = pad_ref.shape[0]
    batch_ref[mine, :width] = own_rows_ref[...]
    spread(pad_ref, 0, summary_ref, blocks)
    pick = one_hot(
        (row_x * 2 + row_x) * capacity, capacity, block_len, sent_targets(inn_ref, 0, blocks)
    )
    batch_ref[mine, width:] = place(pick, pad_ref).astype(BF16)
    spread(pad_ref, 0, other_off_ref, blocks // 2)
    spread(pad_ref, blocks // 2, other_inn_ref, blocks // 2)
    pick = one_hot(
        (row_x * 2 + 1 - row_x) * capacity,
        capacity,
        block_len,
        sent_targets(other_inn_ref, 0, blocks),
    )
    batch_ref[theirs, :width] = place(pick, pad_ref).astype(BF16)
    batch_ref[theirs, width:] = jnp.zeros((capacity, width), BF16)


VMEM = pl.BlockSpec(memory_space=pltpu.VMEM)
SMEM = pl.BlockSpec(memory_space=pltpu.SMEM)
HBM = pl.BlockSpec(memory_space=pltpu.HBM)
SDS = jax.ShapeDtypeStruct


def in_hbm(*arrays):
    return tuple(pltpu.with_memory_space_constraint(a, pltpu.HBM) for a in arrays)


def on_device(
    agents,
    block_fill,
    neighbours,
    target_slot,
    attention_in,
    attention_out,
    policy_in,
    policy_mid,
    policy_out,
):
    blocks_x, blocks_y, block_len, width = agents.shape
    all_blocks = blocks_x * blocks_y
    owners = lax.axis_size("gx")
    count_y = lax.axis_size("gy")
    row_x = lax.axis_index("gx")
    capacity = 3 * all_blocks * block_len // (4 * owners)
    hidden = policy_in.shape[1]
    acts = policy_out.shape[1]
    slots = all_blocks * LIVE
    half_rows = slots // 2
    rows = owners * capacity
    block_fill, neighbours = in_hbm(block_fill, neighbours)
    where = jnp.stack([row_x, lax.axis_index("gy")]).astype(jnp.int32)

    swap = [(0, 1), (1, 0)]
    across = [(i, i - 1) for i in range(2, count_y, 2)]
    across += [(i, i + 1) for i in range(1, count_y - 1, 2)]
    beside = [(i, i ^ 1) for i in range(count_y)]
    diagonal = [
        (g * count_y + a, (1 - g) * count_y + b) for g in range(owners) for a, b in across
    ]

    off, inn = pl.pallas_call(
        stage_kernel,
        out_shape=(SDS((half_rows, width), BF16), SDS((half_rows + TARGET_ROWS, width), BF16)),
        in_specs=[SMEM, HBM, HBM],
        out_specs=(VMEM, VMEM),
        scratch_shapes=[
            pltpu.VMEM((blocks_x, blocks_y, block_len), jnp.int32),
            pltpu.SemaphoreType.DMA((3, blocks_x)),
        ],
        compiler_params=pltpu.CompilerParams(vmem_limit_bytes=4 * MIB),
        name="stage",
    )(where, *in_hbm(target_slot, agents))
    other_inn = lax.ppermute(inn, "gx", swap)
    other_off = lax.ppermute(off, "gx", swap)
    side_off = lax.ppermute(off, "gy", across)
    side_inn = lax.ppermute(inn, "gy", beside)
    attention_in, attention_out, own_rows, pick_out, table, token = pl.pallas_call(
        local_kernel,
        out_shape=(
            SDS(attention_in.shape, BF16),
            SDS(attention_out.shape, BF16),
            SDS((capacity, width), BF16),
            SDS((capacity, all_blocks * block_len), BF16),
            SDS((all_blocks, 2 * neighbours.shape[2] + 2), jnp.int32),
            SDS((8, 128), F32),
        ),
        in_specs=[SMEM] * 3 + [VMEM] * 2 + [HBM] * 2,
        out_specs=(VMEM,) * 4 + (SMEM, VMEM),
        scratch_shapes=[
            pltpu.VMEM((all_blocks, block_len, width), BF16),
            pltpu.SemaphoreType.DMA((3,)),
        ],
        compiler_params=pltpu.CompilerParams(vmem_limit_bytes=8 * MIB),
        cost_estimate=pl.CostEstimate(
            flops=2 * capacity * all_blocks * block_len * width,
            bytes_accessed=8 * MIB,
            transcendentals=0,
        ),
        name="local",
    )(block_fill, neighbours, where, off, inn, *in_hbm(attention_in, attention_out))
    other_side_off = lax.ppermute(off, ("gx", "gy"), diagonal)
    other_inn, other_off, side_off, side_inn, other_side_off, token = lax.optimization_barrier(
        (other_inn, other_off, side_off, side_inn, other_side_off, token)
    )
    other_side_inn = lax.ppermute(other_inn, "gy", beside)

    window = blocks_x * owners * (blocks_y + 2 * REACH)
    scores = all_blocks * HEADS * LIVE * 5 * LIVE
    summary, packed = pl.pallas_call(
        attention_kernel,
        out_shape=(SDS((slots, width), BF16), SDS((capacity, width), BF16)),
        in_specs=[SMEM] * 2 + [VMEM] * 12,
        out_specs=(VMEM, VMEM),
        scratch_shapes=[
            pltpu.VMEM((window, LIVE, width), BF16),
            pltpu.VMEM((window, LIVE, width), BF16),
            pltpu.VMEM((slots, width), BF16),
            pltpu.VMEM((all_blocks, block_len, width), BF16),
        ],
        compiler_params=pltpu.CompilerParams(vmem_limit_bytes=16 * MIB),
        cost_estimate=pl.CostEstimate(
            flops=2 * (2 * scores + window * LIVE * 2 * width) * width,
            bytes_accessed=8 * MIB,
            transcendentals=2 * scores,
        ),
        name="attention",
    )(
        table,
        where,
        off,
        inn,
        other_off,
        other_inn,
        side_off,
        side_inn,
        other_side_off,
        other_side_inn,
        attention_in,
        attention_out,
        pick_out,
        token,
    )
    arrived = lax.ppermute(packed, "gx", swap)
    actions, batch = pl.pallas_call(
        policy_kernel,
        out_shape=(
            SDS((blocks_x, blocks_y, block_len, acts), BF16),
            SDS((rows, 2 * width), BF16),
        ),
        in_specs=[SMEM] * 2 + [VMEM] * 9,
        out_specs=(VMEM, VMEM),
        scratch_shapes=[
            pltpu.VMEM((slots, 2 * width), BF16),
            pltpu.VMEM((slots, hidden), BF16),
            pltpu.VMEM((slots, hidden), BF16),
            pltpu.VMEM((all_blocks, block_len, width), BF16),
        ],
        compiler_params=pltpu.CompilerParams(vmem_limit_bytes=16 * MIB),
        cost_estimate=pl.CostEstimate(
            flops=2 * slots * hidden * (2 * width + 2 * hidden + acts),
            bytes_accessed=12 * MIB,
            transcendentals=3 * slots * hidden,
        ),
        name="policy",
    )(
        table,
        where,
        off,
        inn,
        other_off,
        other_inn,
        summary,
        own_rows,
        policy_in,
        policy_mid,
        policy_out,
    )
    batch = lax.dynamic_update_slice(batch, arrived, ((1 - row_x) * capacity, width))
    return actions, batch.reshape(1, 1, rows, 2 * width)


def solution(mesh):
    return jax.shard_map(
        on_device,
        mesh=mesh,
        in_specs=(
            P("gx", "gy", None, None),
            P(),
            P("gx", "gy", None),
            P("gx", "gy", None),
            P(),
            P(),
            P(),
            P(),
            P(),
        ),
        out_specs=(P("gx", "gy", None, None), P("gx", "gy", None, None)),
        check_vma=False,
    )
```

```python
import math

import jax
import jax.numpy as jnp
from jax import lax
from jax.experimental import pallas as pl
from jax.experimental.pallas import tpu as pltpu
from jax.sharding import PartitionSpec as P

HEADS = 4
LIVE = 96
REACH = 2
SCORE_CAP = 30.0
NORM_EPS = 1e-06
LOG2_E = math.log2(math.e)
TARGET_ROWS = 8
MIB = 1 << 20
BF16 = jnp.bfloat16
F32 = jnp.float32


def nt_dot(a, b):
    return lax.dot_general(a, b, (((1,), (1,)), ((), ())), preferred_element_type=F32)


def key_tables(table_ref, fill_ref, near_ref, b, lx, ly, place):
    row_x, row_y, blocks_x, blocks_y = place
    rows_x, rows_y = fill_ref.shape
    columns = blocks_y + 2 * REACH
    key_blocks = near_ref.shape[2] + 1
    home_x = row_x * blocks_x + lx
    home_y = row_y * blocks_y + ly
    table_ref[b, 0] = lx * columns + ly + REACH
    table_ref[b, key_blocks] = fill_ref[home_x, home_y]
    for d in range(key_blocks - 1):
        direction = near_ref[lx, ly, d]
        cell = direction + jnp.where(direction >= 12, 1, 0)
        cell_x = (cell * 13) >> 6
        step_x = cell_x - REACH
        step_y = cell - cell_x * 5 - REACH
        at_x = home_x + step_x
        at_y = home_y + step_y
        inside = (at_x >= 0) & (at_x < rows_x) & (at_y >= 0) & (at_y < rows_y)
        safe_x = jnp.clip(at_x, 0, rows_x - 1)
        safe_y = jnp.clip(at_y, 0, rows_y - 1)
        tile_x = jnp.where(safe_x >= blocks_x, 1, 0)
        other = jnp.where(tile_x == row_x, 0, 1)
        in_x = safe_x - tile_x * blocks_x
        table_ref[b, 1 + d] = (other * blocks_x + in_x) * columns + ly + step_y + REACH
        table_ref[b, key_blocks + 1 + d] = jnp.where(inside, fill_ref[safe_x, safe_y], 0)


def one_hot(base, capacity, block_len, target_rows):
    row = lax.broadcasted_iota(jnp.int32, (capacity, block_len), 0) + base
    row = row.astype(F32)
    return jnp.concatenate(
        [jnp.where(row == target, 1.0, 0.0).astype(BF16) for target in target_rows], axis=1
    )


def place(pick, pad_ref):
    blocks, block_len, width = pad_ref.shape
    flat = pad_ref[...].reshape(blocks * block_len, width)
    return jnp.dot(pick, flat, preferred_element_type=F32)


def sent_targets(ref, first, count):
    start = ref.shape[0] - TARGET_ROWS
    half = ref.shape[1] // 2
    both = ref[start : start + TARGET_ROWS].astype(F32)
    rows = both[:, :half] * 256.0 + both[:, half:]
    return [rows[b : b + 1] for b in range(first, first + count)]


def spread(pad_ref, first, rows, blocks):
    _, block_len, width = pad_ref.shape
    for b in range(blocks):
        pad_ref[first + b, :LIVE] = rows[b * LIVE : (b + 1) * LIVE]
        pad_ref[first + b, LIVE:] = jnp.zeros((block_len - LIVE, width), pad_ref.dtype)


def stage_kernel(place_ref, target_hbm, agents_hbm, off_ref, inn_ref, target_ref, sems):
    blocks_x, _, _, _ = agents_hbm.shape
    core = place_ref[1] & 1
    rows = REACH * LIVE
    targets = pltpu.make_async_copy(target_hbm, target_ref, sems.at[2, 0])
    targets.start()
    copies = []
    for x in range(blocks_x):
        for ref, column, s in ((off_ref, core * REACH, 0), (inn_ref, REACH - core * REACH, 1)):
            copies.append(
                pltpu.make_async_copy(
                    agents_hbm.at[x, pl.ds(column, REACH), pl.ds(0, LIVE)],
                    ref.at[pl.ds(x * rows, rows)].reshape(REACH, LIVE, ref.shape[1]),
                    sems.at[s, x],
                )
            )
    for copy in copies:
        copy.start()
    targets.wait()
    halves = []
    for column in (core * REACH, REACH - core * REACH):
        for x in range(blocks_x):
            for c in range(REACH):
                halves.append(target_ref[x, pl.ds(column + c, 1), :])
    target = jnp.concatenate(halves, axis=0)
    high = target >> 8
    low = target - high * 256
    split = jnp.concatenate([high, low], axis=1).astype(F32).astype(BF16)
    inn_ref[blocks_x * rows :] = split
    for copy in copies:
        copy.wait()


def local_kernel(
    fill_ref,
    near_ref,
    place_ref,
    off_ref,
    inn_ref,
    weight_in_hbm,
    weight_out_hbm,
    weight_in_ref,
    weight_out_ref,
    own_rows_ref,
    pick_out_ref,
    table_ref,
    token_ref,
    pad_ref,
    sems,
):
    copies = [
        pltpu.make_async_copy(weight_in_hbm, weight_in_ref, sems.at[0]),
        pltpu.make_async_copy(weight_out_hbm, weight_out_ref, sems.at[1]),
    ]
    for copy in copies:
        copy.start()
    capacity = own_rows_ref.shape[0]
    blocks, block_len, _ = pad_ref.shape
    row_x = place_ref[0]
    core = place_ref[1] & 1
    place_of = (row_x, place_ref[1], blocks // (2 * REACH), 2 * REACH)
    for half, first in enumerate((core * REACH, REACH - core * REACH)):
        for i in range(blocks // 2):
            b = half * (blocks // 2) + i
            at = (i // REACH, first + i % REACH)
            key_tables(table_ref, fill_ref, near_ref, b, *at, place_of)
    spread(pad_ref, 0, off_ref, blocks // 2)
    spread(pad_ref, blocks // 2, inn_ref, blocks // 2)
    targets = sent_targets(inn_ref, 0, blocks)
    pick_out_ref[...] = one_hot(
        ((1 - row_x) * 2 + row_x) * capacity, capacity, block_len, targets
    )
    pick = one_hot((row_x * 2 + row_x) * capacity, capacity, block_len, targets)
    own_rows_ref[...] = place(pick, pad_ref).astype(BF16)
    token_ref[...] = jnp.zeros_like(token_ref)
    for copy in copies:
        copy.wait()


def others_kernel(place_ref, other_off_ref, other_inn_ref, other_rows_ref, pad_ref):
    capacity = other_rows_ref.shape[0]
    blocks, block_len, _ = pad_ref.shape
    row_x = place_ref[0]
    spread(pad_ref, 0, other_off_ref, blocks // 2)
    spread(pad_ref, blocks // 2, other_inn_ref, blocks // 2)
    pick = one_hot(
        (row_x * 2 + 1 - row_x) * capacity,
        capacity,
        block_len,
        sent_targets(other_inn_ref, 0, blocks),
    )
    other_rows_ref[...] = place(pick, pad_ref).astype(BF16)


def attention_kernel(
    table_ref,
    place_ref,
    off_ref,
    inn_ref,
    other_off_ref,
    other_inn_ref,
    side_off_ref,
    side_inn_ref,
    other_side_off_ref,
    other_side_inn_ref,
    weight_in_ref,
    weight_out_ref,
    pick_out_ref,
    token_ref,
    summary_ref,
    packed_ref,
    keys_ref,
    values_ref,
    context_ref,
    pad_ref,
):
    width = weight_out_ref.shape[0]
    head = width // HEADS
    half_rows = off_ref.shape[0]
    each = half_rows // LIVE
    blocks_x = each // REACH
    columns = 4 * REACH
    core = place_ref[1] & 1
    at_off = REACH + REACH * core
    at_inn = 2 * REACH - REACH * core
    at_side_off = 3 * REACH * core
    at_side_inn = 3 * REACH - 3 * REACH * core
    sources = (
        (0, at_off, off_ref),
        (0, at_inn, inn_ref),
        (1, at_off, other_off_ref),
        (1, at_inn, other_inn_ref),
        (0, at_side_off, side_off_ref),
        (0, at_side_inn, side_inn_ref),
        (1, at_side_off, other_side_off_ref),
        (1, at_side_inn, other_side_inn_ref),
    )
    for o, column, ref in sources:
        rows = ref[:half_rows]
        both = jnp.dot(rows, weight_in_ref[:, width:], preferred_element_type=F32).astype(BF16)
        both = both.reshape(each, LIVE, 2 * width)
        for x in range(blocks_x):
            at = (o * blocks_x + x) * columns + column
            keys_ref[pl.ds(at, REACH)] = both[x * REACH : (x + 1) * REACH, :, :width]
            values_ref[pl.ds(at, REACH)] = both[x * REACH : (x + 1) * REACH, :, width:]

    key_blocks = table_ref.shape[1] // 2
    lane = lax.broadcasted_iota(jnp.int32, (1, key_blocks * LIVE), 1)
    head_of = lax.broadcasted_iota(jnp.int32, (1, width), 1) // head
    queries = [
        jnp.dot(ref[:half_rows], weight_in_ref[:, :width], preferred_element_type=F32).astype(BF16)
        for ref in (off_ref, inn_ref)
    ]
    for b in range(2 * each):
        where_to = [table_ref[b, j] for j in range(key_blocks)]
        counts = [table_ref[b, key_blocks + j] for j in range(key_blocks)]
        i = b % each
        query = queries[b // each][i * LIVE : (i + 1) * LIVE]
        split = jnp.concatenate(
            [jnp.where(head_of == h, query, jnp.zeros_like(query)) for h in range(HEADS)],
            axis=0,
        )
        keys = jnp.concatenate([keys_ref[w] for w in where_to], axis=0)
        values = jnp.concatenate([values_ref[w] for w in where_to], axis=0)
        end = jnp.full(lane.shape, counts[0], jnp.int32)
        for j in range(1, key_blocks):
            end = jnp.where(lane >= j * LIVE, counts[j] + j * LIVE, end)
        raw = nt_dot(split, keys)
        capped = jnp.tanh(raw * (1.0 / (math.sqrt(head) * SCORE_CAP)))
        weight = jnp.exp2(capped * (SCORE_CAP * LOG2_E))
        weight = jnp.where(lane < end, weight, 0.0)
        total = jnp.sum(weight, axis=-1, keepdims=True)
        weight = (weight * (1.0 / total)).astype(BF16)
        mixed = jnp.dot(weight, values, preferred_element_type=F32)
        context = mixed[:LIVE]
        for h in range(1, HEADS):
            context = jnp.where(head_of == h, mixed[h * LIVE : (h + 1) * LIVE], context)
        context_ref[b * LIVE : (b + 1) * LIVE] = context.astype(BF16)
    out = jnp.dot(context_ref[...], weight_out_ref[...], preferred_element_type=F32)
    scale = lax.rsqrt(jnp.mean(out * out, axis=-1, keepdims=True) + NORM_EPS)
    out = (out * scale).astype(BF16)
    summary_ref[...] = out
    spread(pad_ref, 0, out, 2 * each)
    packed_ref[...] = place(pick_out_ref[...], pad_ref).astype(BF16)


def silu(v):
    half = 0.5 * v
    return half + half * jnp.tanh(half)


def policy_kernel(
    table_ref,
    place_ref,
    off_ref,
    inn_ref,
    summary_ref,
    own_rows_ref,
    other_rows_ref,
    policy_in_ref,
    policy_mid_ref,
    policy_out_ref,
    actions_ref,
    batch_ref,
    x_ref,
    h_ref,
    g_ref,
    pad_ref,
):
    width = off_ref.shape[1]
    blocks_x, blocks_y, block_len, _ = actions_ref.shape
    row_x = place_ref[0]
    core = place_ref[1] & 1
    capacity = batch_ref.shape[0] // 2
    half_rows = off_ref.shape[0]
    x_ref[:half_rows, :width] = off_ref[...]
    x_ref[half_rows:, :width] = inn_ref[:half_rows]
    x_ref[:, width:] = summary_ref[...]
    chunk = 256
    hidden = policy_in_ref.shape[1]
    for n in range(0, hidden, chunk):
        v = jnp.dot(x_ref[...], policy_in_ref[:, n : n + chunk], preferred_element_type=F32)
        h_ref[:, n : n + chunk] = silu(v).astype(BF16)
    now, later = h_ref, g_ref
    for m in range(policy_mid_ref.shape[0]):
        for n in range(0, hidden, chunk):
            v = jnp.dot(
                now[...], policy_mid_ref[m, :, n : n + chunk], preferred_element_type=F32
            )
            later[:, n : n + chunk] = silu(v).astype(BF16)
        now, later = later, now
    acts = jnp.dot(now[...], policy_out_ref[...], preferred_element_type=F32)
    slot = lax.broadcasted_iota(jnp.int32, (LIVE, 1), 0)
    for half, first in enumerate((core * REACH, REACH - core * REACH)):
        for i in range(blocks_x * REACH):
            lx = i // REACH
            ly = first + i % REACH
            b = half * blocks_x * REACH + i
            fill = table_ref[b, table_ref.shape[1] // 2]
            act = jnp.where(slot < fill, acts[b * LIVE : (b + 1) * LIVE], 0.0)
            actions_ref[lx, ly, :LIVE] = act.astype(BF16)
            actions_ref[lx, ly, LIVE:] = jnp.zeros((block_len - LIVE, act.shape[1]), BF16)

    mine = pl.ds(pl.multiple_of(row_x * capacity, capacity), capacity)
    theirs = pl.ds(pl.multiple_of((1 - row_x) * capacity, capacity), capacity)
    blocks = pad_ref.shape[0]
    batch_ref[mine, :width] = own_rows_ref[...]
    spread(pad_ref, 0, summary_ref, blocks)
    pick = one_hot(
        (row_x * 2 + row_x) * capacity, capacity, block_len, sent_targets(inn_ref, 0, blocks)
    )
    batch_ref[mine, width:] = place(pick, pad_ref).astype(BF16)
    batch_ref[theirs, :width] = other_rows_ref[...]
    batch_ref[theirs, width:] = jnp.zeros((capacity, width), BF16)


VMEM = pl.BlockSpec(memory_space=pltpu.VMEM)
SMEM = pl.BlockSpec(memory_space=pltpu.SMEM)
HBM = pl.BlockSpec(memory_space=pltpu.HBM)
SDS = jax.ShapeDtypeStruct


def in_hbm(*arrays):
    return tuple(pltpu.with_memory_space_constraint(a, pltpu.HBM) for a in arrays)


def on_device(
    agents,
    block_fill,
    neighbours,
    target_slot,
    attention_in,
    attention_out,
    policy_in,
    policy_mid,
    policy_out,
):
    blocks_x, blocks_y, block_len, width = agents.shape
    all_blocks = blocks_x * blocks_y
    owners = lax.axis_size("gx")
    count_y = lax.axis_size("gy")
    row_x = lax.axis_index("gx")
    capacity = 3 * all_blocks * block_len // (4 * owners)
    hidden = policy_in.shape[1]
    acts = policy_out.shape[1]
    slots = all_blocks * LIVE
    half_rows = slots // 2
    rows = owners * capacity
    block_fill, neighbours = in_hbm(block_fill, neighbours)
    where = jnp.stack([row_x, lax.axis_index("gy")]).astype(jnp.int32)

    swap = [(0, 1), (1, 0)]
    across = [(i, i - 1) for i in range(2, count_y, 2)]
    across += [(i, i + 1) for i in range(1, count_y - 1, 2)]
    beside = [(i, i ^ 1) for i in range(count_y)]
    diagonal = [
        (g * count_y + a, (1 - g) * count_y + b) for g in range(owners) for a, b in across
    ]

    off, inn = pl.pallas_call(
        stage_kernel,
        out_shape=(SDS((half_rows, width), BF16), SDS((half_rows + TARGET_ROWS, width), BF16)),
        in_specs=[SMEM, HBM, HBM],
        out_specs=(VMEM, VMEM),
        scratch_shapes=[
            pltpu.VMEM((blocks_x, blocks_y, block_len), jnp.int32),
            pltpu.SemaphoreType.DMA((3, blocks_x)),
        ],
        compiler_params=pltpu.CompilerParams(vmem_limit_bytes=4 * MIB),
        name="stage",
    )(where, *in_hbm(target_slot, agents))
    other_inn = lax.ppermute(inn, "gx", swap)
    other_off = lax.ppermute(off, "gx", swap)
    side_off = lax.ppermute(off, "gy", across)
    side_inn = lax.ppermute(inn, "gy", beside)
    other_side_off = lax.ppermute(off, ("gx", "gy"), diagonal)
    attention_in, attention_out, own_rows, pick_out, table, token = pl.pallas_call(
        local_kernel,
        out_shape=(
            SDS(attention_in.shape, BF16),
            SDS(attention_out.shape, BF16),
            SDS((capacity, width), BF16),
            SDS((capacity, all_blocks * block_len), BF16),
            SDS((all_blocks, 2 * neighbours.shape[2] + 2), jnp.int32),
            SDS((8, 128), F32),
        ),
        in_specs=[SMEM] * 3 + [VMEM] * 2 + [HBM] * 2,
        out_specs=(VMEM,) * 4 + (SMEM, VMEM),
        scratch_shapes=[
            pltpu.VMEM((all_blocks, block_len, width), BF16),
            pltpu.SemaphoreType.DMA((3,)),
        ],
        compiler_params=pltpu.CompilerParams(vmem_limit_bytes=8 * MIB),
        cost_estimate=pl.CostEstimate(
            flops=2 * capacity * all_blocks * block_len * width,
            bytes_accessed=8 * MIB,
            transcendentals=0,
        ),
        name="local",
    )(block_fill, neighbours, where, off, inn, *in_hbm(attention_in, attention_out))
    token, other_side_off, side_inn, side_off, other_off, other_inn = lax.optimization_barrier(
        (token, other_side_off, side_inn, side_off, other_off, other_inn)
    )
    other_side_inn = lax.ppermute(other_inn, "gy", beside)
    other_rows = pl.pallas_call(
        others_kernel,
        out_shape=SDS((capacity, width), BF16),
        in_specs=[SMEM, VMEM, VMEM],
        out_specs=VMEM,
        scratch_shapes=[pltpu.VMEM((all_blocks, block_len, width), BF16)],
        compiler_params=pltpu.CompilerParams(vmem_limit_bytes=8 * MIB),
        cost_estimate=pl.CostEstimate(
            flops=2 * capacity * all_blocks * block_len * width,
            bytes_accessed=2 * MIB,
            transcendentals=0,
        ),
        name="others",
    )(where, other_off, other_inn)
    other_rows, other_side_inn = lax.optimization_barrier((other_rows, other_side_inn))

    window = blocks_x * owners * (blocks_y + 2 * REACH)
    scores = all_blocks * HEADS * LIVE * 5 * LIVE
    summary, packed = pl.pallas_call(
        attention_kernel,
        out_shape=(SDS((slots, width), BF16), SDS((capacity, width), BF16)),
        in_specs=[SMEM] * 2 + [VMEM] * 12,
        out_specs=(VMEM, VMEM),
        scratch_shapes=[
            pltpu.VMEM((window, LIVE, width), BF16),
            pltpu.VMEM((window, LIVE, width), BF16),
            pltpu.VMEM((slots, width), BF16),
            pltpu.VMEM((all_blocks, block_len, width), BF16),
        ],
        compiler_params=pltpu.CompilerParams(vmem_limit_bytes=16 * MIB),
        cost_estimate=pl.CostEstimate(
            flops=2 * (2 * scores + window * LIVE * 2 * width) * width,
            bytes_accessed=8 * MIB,
            transcendentals=2 * scores,
        ),
        name="attention",
    )(
        table,
        where,
        off,
        inn,
        other_off,
        other_inn,
        side_off,
        side_inn,
        other_side_off,
        other_side_inn,
        attention_in,
        attention_out,
        pick_out,
        token,
    )
    arrived = lax.ppermute(packed, "gx", swap)
    actions, batch = pl.pallas_call(
        policy_kernel,
        out_shape=(
            SDS((blocks_x, blocks_y, block_len, acts), BF16),
            SDS((rows, 2 * width), BF16),
        ),
        in_specs=[SMEM] * 2 + [VMEM] * 8,
        out_specs=(VMEM, VMEM),
        scratch_shapes=[
            pltpu.VMEM((slots, 2 * width), BF16),
            pltpu.VMEM((slots, hidden), BF16),
            pltpu.VMEM((slots, hidden), BF16),
            pltpu.VMEM((all_blocks, block_len, width), BF16),
        ],
        compiler_params=pltpu.CompilerParams(vmem_limit_bytes=16 * MIB),
        cost_estimate=pl.CostEstimate(
            flops=2 * slots * hidden * (2 * width + 2 * hidden + acts),
            bytes_accessed=12 * MIB,
            transcendentals=3 * slots * hidden,
        ),
        name="policy",
    )(
        table,
        where,
        off,
        inn,
        summary,
        own_rows,
        other_rows,
        policy_in,
        policy_mid,
        policy_out,
    )
    batch = lax.dynamic_update_slice(batch, arrived, ((1 - row_x) * capacity, width))
    return actions, batch.reshape(1, 1, rows, 2 * width)


def solution(mesh):
    return jax.shard_map(
        on_device,
        mesh=mesh,
        in_specs=(
            P("gx", "gy", None, None),
            P(),
            P("gx", "gy", None),
            P("gx", "gy", None),
            P(),
            P(),
            P(),
            P(),
            P(),
        ),
        out_specs=(P("gx", "gy", None, None), P("gx", "gy", None, None)),
        check_vma=False,
    )
```

```python
import math

import jax
import jax.numpy as jnp
from jax import lax
from jax.experimental import pallas as pl
from jax.experimental.pallas import tpu as pltpu
from jax.sharding import PartitionSpec as P

HEADS = 4
LIVE = 96
REACH = 2
SCORE_CAP = 30.0
NORM_EPS = 1e-06
LOG2_E = math.log2(math.e)
TARGET_ROWS = 8
MIB = 1 << 20
BF16 = jnp.bfloat16
F32 = jnp.float32


def nt_dot(a, b):
    return lax.dot_general(a, b, (((1,), (1,)), ((), ())), preferred_element_type=F32)


def key_tables(table_ref, fill_ref, near_ref, b, lx, ly, place):
    row_x, row_y, blocks_x, blocks_y = place
    rows_x, rows_y = fill_ref.shape
    columns = blocks_y + 2 * REACH
    key_blocks = near_ref.shape[2] + 1
    home_x = row_x * blocks_x + lx
    home_y = row_y * blocks_y + ly
    table_ref[b, 0] = lx * columns + ly + REACH
    table_ref[b, key_blocks] = fill_ref[home_x, home_y]
    for d in range(key_blocks - 1):
        direction = near_ref[lx, ly, d]
        cell = direction + jnp.where(direction >= 12, 1, 0)
        cell_x = (cell * 13) >> 6
        step_x = cell_x - REACH
        step_y = cell - cell_x * 5 - REACH
        at_x = home_x + step_x
        at_y = home_y + step_y
        inside = (at_x >= 0) & (at_x < rows_x) & (at_y >= 0) & (at_y < rows_y)
        safe_x = jnp.clip(at_x, 0, rows_x - 1)
        safe_y = jnp.clip(at_y, 0, rows_y - 1)
        tile_x = jnp.where(safe_x >= blocks_x, 1, 0)
        other = jnp.where(tile_x == row_x, 0, 1)
        in_x = safe_x - tile_x * blocks_x
        table_ref[b, 1 + d] = (other * blocks_x + in_x) * columns + ly + step_y + REACH
        table_ref[b, key_blocks + 1 + d] = jnp.where(inside, fill_ref[safe_x, safe_y], 0)


def one_hot(base, capacity, block_len, target_rows):
    row = lax.broadcasted_iota(jnp.int32, (capacity, block_len), 0) + base
    row = row.astype(F32)
    return jnp.concatenate(
        [jnp.where(row == target, 1.0, 0.0).astype(BF16) for target in target_rows], axis=1
    )


def place(pick, pad_ref):
    blocks, block_len, width = pad_ref.shape
    flat = pad_ref[...].reshape(blocks * block_len, width)
    return jnp.dot(pick, flat, preferred_element_type=F32)


def sent_targets(ref, first, count):
    start = ref.shape[0] - TARGET_ROWS
    half = ref.shape[1] // 2
    both = ref[start : start + TARGET_ROWS].astype(F32)
    rows = both[:, :half] * 256.0 + both[:, half:]
    return [rows[b : b + 1] for b in range(first, first + count)]


def spread(pad_ref, first, rows, blocks):
    _, block_len, width = pad_ref.shape
    for b in range(blocks):
        pad_ref[first + b, :LIVE] = rows[b * LIVE : (b + 1) * LIVE]
        pad_ref[first + b, LIVE:] = jnp.zeros((block_len - LIVE, width), pad_ref.dtype)


def stage_kernel(target_hbm, agents_hbm, off_ref, inn_ref, target_ref, sems):
    blocks_x, _, _, _ = agents_hbm.shape
    core = lax.axis_index("gy") & 1
    rows = REACH * LIVE
    targets = pltpu.make_async_copy(target_hbm, target_ref, sems.at[2, 0])
    targets.start()
    copies = []
    for x in range(blocks_x):
        for ref, column, s in ((off_ref, core * REACH, 0), (inn_ref, REACH - core * REACH, 1)):
            copies.append(
                pltpu.make_async_copy(
                    agents_hbm.at[x, pl.ds(column, REACH), pl.ds(0, LIVE)],
                    ref.at[pl.ds(x * rows, rows)].reshape(REACH, LIVE, ref.shape[1]),
                    sems.at[s, x],
                )
            )
    for copy in copies:
        copy.start()
    targets.wait()
    halves = []
    for column in (core * REACH, REACH - core * REACH):
        for x in range(blocks_x):
            for c in range(REACH):
                halves.append(target_ref[x, pl.ds(column + c, 1), :])
    target = jnp.concatenate(halves, axis=0)
    high = target >> 8
    low = target - high * 256
    split = jnp.concatenate([high, low], axis=1).astype(F32).astype(BF16)
    inn_ref[blocks_x * rows :] = split
    for copy in copies:
        copy.wait()


def local_kernel(
    fill_ref,
    near_ref,
    off_ref,
    inn_ref,
    weight_in_hbm,
    weight_out_hbm,
    weight_in_ref,
    weight_out_ref,
    own_rows_ref,
    pick_out_ref,
    table_ref,
    token_ref,
    pad_ref,
    sems,
):
    copies = [
        pltpu.make_async_copy(weight_in_hbm, weight_in_ref, sems.at[0]),
        pltpu.make_async_copy(weight_out_hbm, weight_out_ref, sems.at[1]),
    ]
    for copy in copies:
        copy.start()
    capacity = own_rows_ref.shape[0]
    blocks, block_len, _ = pad_ref.shape
    row_x = lax.axis_index("gx")
    core = lax.axis_index("gy") & 1
    place_of = (row_x, lax.axis_index("gy"), blocks // (2 * REACH), 2 * REACH)
    for half, first in enumerate((core * REACH, REACH - core * REACH)):
        for i in range(blocks // 2):
            b = half * (blocks // 2) + i
            at = (i // REACH, first + i % REACH)
            key_tables(table_ref, fill_ref, near_ref, b, *at, place_of)
    spread(pad_ref, 0, off_ref, blocks // 2)
    spread(pad_ref, blocks // 2, inn_ref, blocks // 2)
    targets = sent_targets(inn_ref, 0, blocks)
    pick_out_ref[...] = one_hot(
        ((1 - row_x) * 2 + row_x) * capacity, capacity, block_len, targets
    )
    pick = one_hot((row_x * 2 + row_x) * capacity, capacity, block_len, targets)
    own_rows_ref[...] = place(pick, pad_ref).astype(BF16)
    token_ref[...] = jnp.zeros_like(token_ref)
    for copy in copies:
        copy.wait()


def others_kernel(other_off_ref, other_inn_ref, other_rows_ref, pad_ref):
    capacity = other_rows_ref.shape[0]
    blocks, block_len, _ = pad_ref.shape
    row_x = lax.axis_index("gx")
    spread(pad_ref, 0, other_off_ref, blocks // 2)
    spread(pad_ref, blocks // 2, other_inn_ref, blocks // 2)
    pick = one_hot(
        (row_x * 2 + 1 - row_x) * capacity,
        capacity,
        block_len,
        sent_targets(other_inn_ref, 0, blocks),
    )
    other_rows_ref[...] = place(pick, pad_ref).astype(BF16)


def attention_kernel(
    table_ref,
    off_ref,
    inn_ref,
    other_off_ref,
    other_inn_ref,
    side_off_ref,
    side_inn_ref,
    other_side_off_ref,
    other_side_inn_ref,
    weight_in_ref,
    weight_out_ref,
    pick_out_ref,
    token_ref,
    summary_ref,
    packed_ref,
    keys_ref,
    values_ref,
    context_ref,
    pad_ref,
):
    width = weight_out_ref.shape[0]
    head = width // HEADS
    half_rows = off_ref.shape[0]
    each = half_rows // LIVE
    blocks_x = each // REACH
    columns = 4 * REACH
    core = lax.axis_index("gy") & 1
    at_off = REACH + REACH * core
    at_inn = 2 * REACH - REACH * core
    at_side_off = 3 * REACH * core
    at_side_inn = 3 * REACH - 3 * REACH * core
    sources = (
        (0, at_off, off_ref),
        (0, at_inn, inn_ref),
        (1, at_off, other_off_ref),
        (1, at_inn, other_inn_ref),
        (0, at_side_off, side_off_ref),
        (0, at_side_inn, side_inn_ref),
        (1, at_side_off, other_side_off_ref),
        (1, at_side_inn, other_side_inn_ref),
    )
    for o, column, ref in sources:
        rows = ref[:half_rows]
        both = jnp.dot(rows, weight_in_ref[:, width:], preferred_element_type=F32).astype(BF16)
        both = both.reshape(each, LIVE, 2 * width)
        for x in range(blocks_x):
            at = (o * blocks_x + x) * columns + column
            keys_ref[pl.ds(at, REACH)] = both[x * REACH : (x + 1) * REACH, :, :width]
            values_ref[pl.ds(at, REACH)] = both[x * REACH : (x + 1) * REACH, :, width:]

    key_blocks = table_ref.shape[1] // 2
    lane = lax.broadcasted_iota(jnp.int32, (1, key_blocks * LIVE), 1)
    head_of = lax.broadcasted_iota(jnp.int32, (1, width), 1) // head
    queries = [
        jnp.dot(ref[:half_rows], weight_in_ref[:, :width], preferred_element_type=F32).astype(BF16)
        for ref in (off_ref, inn_ref)
    ]
    for b in range(2 * each):
        where_to = [table_ref[b, j] for j in range(key_blocks)]
        counts = [table_ref[b, key_blocks + j] for j in range(key_blocks)]
        i = b % each
        query = queries[b // each][i * LIVE : (i + 1) * LIVE]
        split = jnp.concatenate(
            [jnp.where(head_of == h, query, jnp.zeros_like(query)) for h in range(HEADS)],
            axis=0,
        )
        keys = jnp.concatenate([keys_ref[w] for w in where_to], axis=0)
        values = jnp.concatenate([values_ref[w] for w in where_to], axis=0)
        end = jnp.full(lane.shape, counts[0], jnp.int32)
        for j in range(1, key_blocks):
            end = jnp.where(lane >= j * LIVE, counts[j] + j * LIVE, end)
        raw = nt_dot(split, keys)
        capped = jnp.tanh(raw * (1.0 / (math.sqrt(head) * SCORE_CAP)))
        weight = jnp.exp2(capped * (SCORE_CAP * LOG2_E))
        weight = jnp.where(lane < end, weight, 0.0)
        total = jnp.sum(weight, axis=-1, keepdims=True)
        weight = (weight * (1.0 / total)).astype(BF16)
        mixed = jnp.dot(weight, values, preferred_element_type=F32)
        context = mixed[:LIVE]
        for h in range(1, HEADS):
            context = jnp.where(head_of == h, mixed[h * LIVE : (h + 1) * LIVE], context)
        context_ref[b * LIVE : (b + 1) * LIVE] = context.astype(BF16)
    out = jnp.dot(context_ref[...], weight_out_ref[...], preferred_element_type=F32)
    scale = lax.rsqrt(jnp.mean(out * out, axis=-1, keepdims=True) + NORM_EPS)
    out = (out * scale).astype(BF16)
    summary_ref[...] = out
    spread(pad_ref, 0, out, 2 * each)
    packed_ref[...] = place(pick_out_ref[...], pad_ref).astype(BF16)


def silu(v):
    half = 0.5 * v
    return half + half * jnp.tanh(half)


def policy_kernel(
    table_ref,
    off_ref,
    inn_ref,
    summary_ref,
    own_rows_ref,
    other_rows_ref,
    policy_in_ref,
    policy_mid_ref,
    policy_out_ref,
    actions_ref,
    batch_ref,
    x_ref,
    h_ref,
    g_ref,
    pad_ref,
):
    width = off_ref.shape[1]
    blocks_x, blocks_y, block_len, _ = actions_ref.shape
    row_x = lax.axis_index("gx")
    core = lax.axis_index("gy") & 1
    capacity = batch_ref.shape[0] // 2
    half_rows = off_ref.shape[0]
    x_ref[:half_rows, :width] = off_ref[...]
    x_ref[half_rows:, :width] = inn_ref[:half_rows]
    x_ref[:, width:] = summary_ref[...]
    chunk = 256
    hidden = policy_in_ref.shape[1]
    for n in range(0, hidden, chunk):
        v = jnp.dot(x_ref[...], policy_in_ref[:, n : n + chunk], preferred_element_type=F32)
        h_ref[:, n : n + chunk] = silu(v).astype(BF16)
    now, later = h_ref, g_ref
    for m in range(policy_mid_ref.shape[0]):
        for n in range(0, hidden, chunk):
            v = jnp.dot(
                now[...], policy_mid_ref[m, :, n : n + chunk], preferred_element_type=F32
            )
            later[:, n : n + chunk] = silu(v).astype(BF16)
        now, later = later, now
    acts = jnp.dot(now[...], policy_out_ref[...], preferred_element_type=F32)
    slot = lax.broadcasted_iota(jnp.int32, (LIVE, 1), 0)
    for half, first in enumerate((core * REACH, REACH - core * REACH)):
        for i in range(blocks_x * REACH):
            lx = i // REACH
            ly = first + i % REACH
            b = half * blocks_x * REACH + i
            fill = table_ref[b, table_ref.shape[1] // 2]
            act = jnp.where(slot < fill, acts[b * LIVE : (b + 1) * LIVE], 0.0)
            actions_ref[lx, ly, :LIVE] = act.astype(BF16)
            actions_ref[lx, ly, LIVE:] = jnp.zeros((block_len - LIVE, act.shape[1]), BF16)

    mine = pl.ds(pl.multiple_of(row_x * capacity, capacity), capacity)
    theirs = pl.ds(pl.multiple_of((1 - row_x) * capacity, capacity), capacity)
    blocks = pad_ref.shape[0]
    batch_ref[mine, :width] = own_rows_ref[...]
    spread(pad_ref, 0, summary_ref, blocks)
    pick = one_hot(
        (row_x * 2 + row_x) * capacity, capacity, block_len, sent_targets(inn_ref, 0, blocks)
    )
    batch_ref[mine, width:] = place(pick, pad_ref).astype(BF16)
    batch_ref[theirs, :width] = other_rows_ref[...]
    batch_ref[theirs, width:] = jnp.zeros((capacity, width), BF16)


VMEM = pl.BlockSpec(memory_space=pltpu.VMEM)
SMEM = pl.BlockSpec(memory_space=pltpu.SMEM)
HBM = pl.BlockSpec(memory_space=pltpu.HBM)
SDS = jax.ShapeDtypeStruct


def in_hbm(*arrays):
    return tuple(pltpu.with_memory_space_constraint(a, pltpu.HBM) for a in arrays)


def on_device(
    agents,
    block_fill,
    neighbours,
    target_slot,
    attention_in,
    attention_out,
    policy_in,
    policy_mid,
    policy_out,
):
    blocks_x, blocks_y, block_len, width = agents.shape
    all_blocks = blocks_x * blocks_y
    owners = lax.axis_size("gx")
    count_y = lax.axis_size("gy")
    row_x = lax.axis_index("gx")
    capacity = 3 * all_blocks * block_len // (4 * owners)
    hidden = policy_in.shape[1]
    acts = policy_out.shape[1]
    slots = all_blocks * LIVE
    half_rows = slots // 2
    rows = owners * capacity
    block_fill, neighbours = in_hbm(block_fill, neighbours)

    swap = [(0, 1), (1, 0)]
    across = [(i, i - 1) for i in range(2, count_y, 2)]
    across += [(i, i + 1) for i in range(1, count_y - 1, 2)]
    beside = [(i, i ^ 1) for i in range(count_y)]
    diagonal = [
        (g * count_y + a, (1 - g) * count_y + b) for g in range(owners) for a, b in across
    ]

    off, inn = pl.pallas_call(
        stage_kernel,
        out_shape=(SDS((half_rows, width), BF16), SDS((half_rows + TARGET_ROWS, width), BF16)),
        in_specs=[HBM, HBM],
        out_specs=(VMEM, VMEM),
        scratch_shapes=[
            pltpu.VMEM((blocks_x, blocks_y, block_len), jnp.int32),
            pltpu.SemaphoreType.DMA((3, blocks_x)),
        ],
        compiler_params=pltpu.CompilerParams(vmem_limit_bytes=4 * MIB),
        name="stage",
    )(*in_hbm(target_slot, agents))
    other_inn = lax.ppermute(inn, "gx", swap)
    other_off = lax.ppermute(off, "gx", swap)
    side_off = lax.ppermute(off, "gy", across)
    side_inn = lax.ppermute(inn, "gy", beside)
    other_side_off = lax.ppermute(off, ("gx", "gy"), diagonal)
    attention_in, attention_out, own_rows, pick_out, table, token = pl.pallas_call(
        local_kernel,
        out_shape=(
            SDS(attention_in.shape, BF16),
            SDS(attention_out.shape, BF16),
            SDS((capacity, width), BF16),
            SDS((capacity, all_blocks * block_len), BF16),
            SDS((all_blocks, 2 * neighbours.shape[2] + 2), jnp.int32),
            SDS((8, 128), F32),
        ),
        in_specs=[SMEM] * 2 + [VMEM] * 2 + [HBM] * 2,
        out_specs=(VMEM,) * 4 + (SMEM, VMEM),
        scratch_shapes=[
            pltpu.VMEM((all_blocks, block_len, width), BF16),
            pltpu.SemaphoreType.DMA((3,)),
        ],
        compiler_params=pltpu.CompilerParams(vmem_limit_bytes=8 * MIB),
        cost_estimate=pl.CostEstimate(
            flops=2 * capacity * all_blocks * block_len * width,
            bytes_accessed=8 * MIB,
            transcendentals=0,
        ),
        name="local",
    )(block_fill, neighbours, off, inn, *in_hbm(attention_in, attention_out))
    other_inn, other_off, side_off, side_inn, other_side_off, token = lax.optimization_barrier(
        (other_inn, other_off, side_off, side_inn, other_side_off, token)
    )
    other_side_inn = lax.ppermute(other_inn, "gy", beside)
    other_rows = pl.pallas_call(
        others_kernel,
        out_shape=SDS((capacity, width), BF16),
        in_specs=[VMEM, VMEM],
        out_specs=VMEM,
        scratch_shapes=[pltpu.VMEM((all_blocks, block_len, width), BF16)],
        compiler_params=pltpu.CompilerParams(vmem_limit_bytes=8 * MIB),
        cost_estimate=pl.CostEstimate(
            flops=2 * capacity * all_blocks * block_len * width,
            bytes_accessed=2 * MIB,
            transcendentals=0,
        ),
        name="others",
    )(other_off, other_inn)
    other_rows, other_side_inn = lax.optimization_barrier((other_rows, other_side_inn))

    window = blocks_x * owners * (blocks_y + 2 * REACH)
    scores = all_blocks * HEADS * LIVE * 5 * LIVE
    summary, packed = pl.pallas_call(
        attention_kernel,
        out_shape=(SDS((slots, width), BF16), SDS((capacity, width), BF16)),
        in_specs=[SMEM] + [VMEM] * 12,
        out_specs=(VMEM, VMEM),
        scratch_shapes=[
            pltpu.VMEM((window, LIVE, width), BF16),
            pltpu.VMEM((window, LIVE, width), BF16),
            pltpu.VMEM((slots, width), BF16),
            pltpu.VMEM((all_blocks, block_len, width), BF16),
        ],
        compiler_params=pltpu.CompilerParams(vmem_limit_bytes=16 * MIB),
        cost_estimate=pl.CostEstimate(
            flops=2 * (2 * scores + window * LIVE * 2 * width) * width,
            bytes_accessed=8 * MIB,
            transcendentals=2 * scores,
        ),
        name="attention",
    )(
        table,
        off,
        inn,
        other_off,
        other_inn,
        side_off,
        side_inn,
        other_side_off,
        other_side_inn,
        attention_in,
        attention_out,
        pick_out,
        token,
    )
    arrived = lax.ppermute(packed, "gx", swap)
    actions, batch = pl.pallas_call(
        policy_kernel,
        out_shape=(
            SDS((blocks_x, blocks_y, block_len, acts), BF16),
            SDS((rows, 2 * width), BF16),
        ),
        in_specs=[SMEM] + [VMEM] * 8,
        out_specs=(VMEM, VMEM),
        scratch_shapes=[
            pltpu.VMEM((slots, 2 * width), BF16),
            pltpu.VMEM((slots, hidden), BF16),
            pltpu.VMEM((slots, hidden), BF16),
            pltpu.VMEM((all_blocks, block_len, width), BF16),
        ],
        compiler_params=pltpu.CompilerParams(vmem_limit_bytes=16 * MIB),
        cost_estimate=pl.CostEstimate(
            flops=2 * slots * hidden * (2 * width + 2 * hidden + acts),
            bytes_accessed=12 * MIB,
            transcendentals=3 * slots * hidden,
        ),
        name="policy",
    )(
        table,
        off,
        inn,
        summary,
        own_rows,
        other_rows,
        policy_in,
        policy_mid,
        policy_out,
    )
    batch = lax.dynamic_update_slice(batch, arrived, ((1 - row_x) * capacity, width))
    return actions, batch.reshape(1, 1, rows, 2 * width)


def solution(mesh):
    return jax.shard_map(
        on_device,
        mesh=mesh,
        in_specs=(
            P("gx", "gy", None, None),
            P(),
            P("gx", "gy", None),
            P("gx", "gy", None),
            P(),
            P(),
            P(),
            P(),
            P(),
        ),
        out_specs=(P("gx", "gy", None, None), P("gx", "gy", None, None)),
        check_vma=False,
    )
```

```python
import math

import jax
import jax.numpy as jnp
from jax import lax
from jax.experimental import pallas as pl
from jax.experimental.pallas import tpu as pltpu
from jax.sharding import PartitionSpec as P

HEADS = 4
LIVE = 96
REACH = 2
SCORE_CAP = 30.0
NORM_EPS = 1e-06
LOG2_E = math.log2(math.e)
TARGET_ROWS = 8
MIB = 1 << 20
BF16 = jnp.bfloat16
F32 = jnp.float32


def nt_dot(a, b):
    return lax.dot_general(a, b, (((1,), (1,)), ((), ())), preferred_element_type=F32)


def key_tables(table_ref, fill_ref, near_ref, b, lx, ly, place):
    row_x, row_y, blocks_x, blocks_y = place
    rows_x, rows_y = fill_ref.shape
    columns = blocks_y + 2 * REACH
    key_blocks = near_ref.shape[2] + 1
    home_x = row_x * blocks_x + lx
    home_y = row_y * blocks_y + ly
    table_ref[b, 0] = lx * columns + ly + REACH
    table_ref[b, key_blocks] = fill_ref[home_x, home_y]
    for d in range(key_blocks - 1):
        direction = near_ref[lx, ly, d]
        cell = direction + jnp.where(direction >= 12, 1, 0)
        cell_x = (cell * 13) >> 6
        step_x = cell_x - REACH
        step_y = cell - cell_x * 5 - REACH
        at_x = home_x + step_x
        at_y = home_y + step_y
        inside = (at_x >= 0) & (at_x < rows_x) & (at_y >= 0) & (at_y < rows_y)
        safe_x = jnp.clip(at_x, 0, rows_x - 1)
        safe_y = jnp.clip(at_y, 0, rows_y - 1)
        tile_x = jnp.where(safe_x >= blocks_x, 1, 0)
        other = jnp.where(tile_x == row_x, 0, 1)
        in_x = safe_x - tile_x * blocks_x
        table_ref[b, 1 + d] = (other * blocks_x + in_x) * columns + ly + step_y + REACH
        table_ref[b, key_blocks + 1 + d] = jnp.where(inside, fill_ref[safe_x, safe_y], 0)


def one_hot(base, capacity, block_len, target_rows):
    row = lax.broadcasted_iota(jnp.int32, (capacity, block_len), 0) + base
    row = row.astype(F32)
    return jnp.concatenate(
        [jnp.where(row == target, 1.0, 0.0).astype(BF16) for target in target_rows], axis=1
    )


def place(pick, pad_ref):
    blocks, block_len, width = pad_ref.shape
    flat = pad_ref[...].reshape(blocks * block_len, width)
    return jnp.dot(pick, flat, preferred_element_type=F32)


def sent_targets(ref, first, count):
    start = ref.shape[0] - TARGET_ROWS
    half = ref.shape[1] // 2
    both = ref[start : start + TARGET_ROWS].astype(F32)
    rows = both[:, :half] * 256.0 + both[:, half:]
    return [rows[b : b + 1] for b in range(first, first + count)]


def spread(pad_ref, first, rows, blocks):
    _, block_len, width = pad_ref.shape
    for b in range(blocks):
        pad_ref[first + b, :LIVE] = rows[b * LIVE : (b + 1) * LIVE]
        pad_ref[first + b, LIVE:] = jnp.zeros((block_len - LIVE, width), pad_ref.dtype)


def stage_kernel(target_hbm, agents_hbm, off_ref, inn_ref, target_ref, sems):
    blocks_x, _, _, _ = agents_hbm.shape
    core = lax.axis_index("gy") & 1
    rows = REACH * LIVE
    targets = pltpu.make_async_copy(target_hbm, target_ref, sems.at[2, 0])
    targets.start()
    copies = []
    for x in range(blocks_x):
        for ref, column, s in ((off_ref, core * REACH, 0), (inn_ref, REACH - core * REACH, 1)):
            copies.append(
                pltpu.make_async_copy(
                    agents_hbm.at[x, pl.ds(column, REACH), pl.ds(0, LIVE)],
                    ref.at[pl.ds(x * rows, rows)].reshape(REACH, LIVE, ref.shape[1]),
                    sems.at[s, x],
                )
            )
    for copy in copies:
        copy.start()
    targets.wait()
    halves = []
    for column in (core * REACH, REACH - core * REACH):
        for x in range(blocks_x):
            for c in range(REACH):
                halves.append(target_ref[x, pl.ds(column + c, 1), :])
    target = jnp.concatenate(halves, axis=0)
    high = target >> 8
    low = target - high * 256
    split = jnp.concatenate([high, low], axis=1).astype(F32).astype(BF16)
    inn_ref[blocks_x * rows :] = split
    for copy in copies:
        copy.wait()


def local_kernel(
    fill_ref,
    near_ref,
    off_ref,
    inn_ref,
    weight_in_hbm,
    weight_out_hbm,
    weight_in_ref,
    weight_out_ref,
    own_rows_ref,
    pick_out_ref,
    table_ref,
    token_ref,
    pad_ref,
    sems,
):
    copies = [
        pltpu.make_async_copy(weight_in_hbm, weight_in_ref, sems.at[0]),
        pltpu.make_async_copy(weight_out_hbm, weight_out_ref, sems.at[1]),
    ]
    for copy in copies:
        copy.start()
    capacity = own_rows_ref.shape[0]
    blocks, block_len, _ = pad_ref.shape
    row_x = lax.axis_index("gx")
    core = lax.axis_index("gy") & 1
    place_of = (row_x, lax.axis_index("gy"), blocks // (2 * REACH), 2 * REACH)
    for half, first in enumerate((core * REACH, REACH - core * REACH)):
        for i in range(blocks // 2):
            b = half * (blocks // 2) + i
            at = (i // REACH, first + i % REACH)
            key_tables(table_ref, fill_ref, near_ref, b, *at, place_of)
    spread(pad_ref, 0, off_ref, blocks // 2)
    spread(pad_ref, blocks // 2, inn_ref, blocks // 2)
    targets = sent_targets(inn_ref, 0, blocks)
    pick_out_ref[...] = one_hot(
        ((1 - row_x) * 2 + row_x) * capacity, capacity, block_len, targets
    )
    pick = one_hot((row_x * 2 + row_x) * capacity, capacity, block_len, targets)
    own_rows_ref[...] = place(pick, pad_ref).astype(BF16)
    token_ref[...] = jnp.zeros_like(token_ref)
    for copy in copies:
        copy.wait()


def others_kernel(other_off_ref, other_inn_ref, other_rows_ref, pad_ref):
    capacity = other_rows_ref.shape[0]
    blocks, block_len, _ = pad_ref.shape
    row_x = lax.axis_index("gx")
    spread(pad_ref, 0, other_off_ref, blocks // 2)
    spread(pad_ref, blocks // 2, other_inn_ref, blocks // 2)
    pick = one_hot(
        (row_x * 2 + 1 - row_x) * capacity,
        capacity,
        block_len,
        sent_targets(other_inn_ref, 0, blocks),
    )
    other_rows_ref[...] = place(pick, pad_ref).astype(BF16)


def attention_kernel(
    table_ref,
    off_ref,
    inn_ref,
    other_off_ref,
    other_inn_ref,
    side_off_ref,
    side_inn_ref,
    other_side_off_ref,
    other_side_inn_ref,
    weight_in_ref,
    weight_out_ref,
    pick_out_ref,
    token_ref,
    summary_ref,
    packed_ref,
    keys_ref,
    values_ref,
    context_ref,
    pad_ref,
):
    width = weight_out_ref.shape[0]
    head = width // HEADS
    half_rows = off_ref.shape[0]
    each = half_rows // LIVE
    blocks_x = each // REACH
    columns = 4 * REACH
    core = lax.axis_index("gy") & 1
    at_off = REACH + REACH * core
    at_inn = 2 * REACH - REACH * core
    at_side_off = 3 * REACH * core
    at_side_inn = 3 * REACH - 3 * REACH * core
    sources = (
        (0, at_off, off_ref),
        (0, at_inn, inn_ref),
        (1, at_off, other_off_ref),
        (1, at_inn, other_inn_ref),
        (0, at_side_off, side_off_ref),
        (0, at_side_inn, side_inn_ref),
        (1, at_side_off, other_side_off_ref),
        (1, at_side_inn, other_side_inn_ref),
    )
    for o, column, ref in sources:
        rows = ref[:half_rows]
        both = jnp.dot(rows, weight_in_ref[:, width:], preferred_element_type=F32).astype(BF16)
        both = both.reshape(each, LIVE, 2 * width)
        for x in range(blocks_x):
            at = (o * blocks_x + x) * columns + column
            keys_ref[pl.ds(at, REACH)] = both[x * REACH : (x + 1) * REACH, :, :width]
            values_ref[pl.ds(at, REACH)] = both[x * REACH : (x + 1) * REACH, :, width:]

    key_blocks = table_ref.shape[1] // 2
    lane = lax.broadcasted_iota(jnp.int32, (1, key_blocks * LIVE), 1)
    head_of = lax.broadcasted_iota(jnp.int32, (1, width), 1) // head
    queries = [
        jnp.dot(ref[:half_rows], weight_in_ref[:, :width], preferred_element_type=F32).astype(BF16)
        for ref in (off_ref, inn_ref)
    ]
    for b in range(2 * each):
        where_to = [table_ref[b, j] for j in range(key_blocks)]
        counts = [table_ref[b, key_blocks + j] for j in range(key_blocks)]
        i = b % each
        query = queries[b // each][i * LIVE : (i + 1) * LIVE]
        split = jnp.concatenate(
            [jnp.where(head_of == h, query, jnp.zeros_like(query)) for h in range(HEADS)],
            axis=0,
        )
        keys = jnp.concatenate([keys_ref[w] for w in where_to], axis=0)
        values = jnp.concatenate([values_ref[w] for w in where_to], axis=0)
        end = jnp.full(lane.shape, counts[0], jnp.int32)
        for j in range(1, key_blocks):
            end = jnp.where(lane >= j * LIVE, counts[j] + j * LIVE, end)
        raw = nt_dot(split, keys)
        capped = jnp.tanh(raw * (1.0 / (math.sqrt(head) * SCORE_CAP)))
        weight = jnp.exp2(capped * (SCORE_CAP * LOG2_E))
        weight = jnp.where(lane < end, weight, 0.0)
        total = jnp.sum(weight, axis=-1, keepdims=True)
        weight = (weight * (1.0 / total)).astype(BF16)
        mixed = jnp.dot(weight, values, preferred_element_type=F32)
        context = mixed[:LIVE]
        for h in range(1, HEADS):
            context = jnp.where(head_of == h, mixed[h * LIVE : (h + 1) * LIVE], context)
        context_ref[b * LIVE : (b + 1) * LIVE] = context.astype(BF16)
    out = jnp.dot(context_ref[...], weight_out_ref[...], preferred_element_type=F32)
    scale = lax.rsqrt(jnp.mean(out * out, axis=-1, keepdims=True) + NORM_EPS)
    out = (out * scale).astype(BF16)
    summary_ref[...] = out
    spread(pad_ref, 0, out, 2 * each)
    packed_ref[...] = place(pick_out_ref[...], pad_ref).astype(BF16)


def silu(v):
    half = 0.5 * v
    return half + half * jnp.tanh(half)


def policy_kernel(
    table_ref,
    off_ref,
    inn_ref,
    summary_ref,
    own_rows_ref,
    other_rows_ref,
    policy_in_ref,
    policy_mid_ref,
    policy_out_ref,
    actions_ref,
    batch_ref,
    x_ref,
    h_ref,
    g_ref,
    pad_ref,
):
    width = off_ref.shape[1]
    blocks_x, blocks_y, block_len, _ = actions_ref.shape
    row_x = lax.axis_index("gx")
    core = lax.axis_index("gy") & 1
    capacity = batch_ref.shape[0] // 2
    half_rows = off_ref.shape[0]
    x_ref[:half_rows, :width] = off_ref[...]
    x_ref[half_rows:, :width] = inn_ref[:half_rows]
    x_ref[:, width:] = summary_ref[...]
    chunk = 256
    hidden = policy_in_ref.shape[1]
    for n in range(0, hidden, chunk):
        v = jnp.dot(x_ref[...], policy_in_ref[:, n : n + chunk], preferred_element_type=F32)
        h_ref[:, n : n + chunk] = silu(v).astype(BF16)
    now, later = h_ref, g_ref
    for m in range(policy_mid_ref.shape[0]):
        for n in range(0, hidden, chunk):
            v = jnp.dot(
                now[...], policy_mid_ref[m, :, n : n + chunk], preferred_element_type=F32
            )
            later[:, n : n + chunk] = silu(v).astype(BF16)
        now, later = later, now
    acts = jnp.dot(now[...], policy_out_ref[...], preferred_element_type=F32)
    slot = lax.broadcasted_iota(jnp.int32, (LIVE, 1), 0)
    for half, first in enumerate((core * REACH, REACH - core * REACH)):
        for i in range(blocks_x * REACH):
            lx = i // REACH
            ly = first + i % REACH
            b = half * blocks_x * REACH + i
            fill = table_ref[b, table_ref.shape[1] // 2]
            act = jnp.where(slot < fill, acts[b * LIVE : (b + 1) * LIVE], 0.0)
            actions_ref[lx, ly, :LIVE] = act.astype(BF16)
            actions_ref[lx, ly, LIVE:] = jnp.zeros((block_len - LIVE, act.shape[1]), BF16)

    mine = pl.ds(pl.multiple_of(row_x * capacity, capacity), capacity)
    theirs = pl.ds(pl.multiple_of((1 - row_x) * capacity, capacity), capacity)
    blocks = pad_ref.shape[0]
    batch_ref[mine, :width] = own_rows_ref[...]
    spread(pad_ref, 0, summary_ref, blocks)
    pick = one_hot(
        (row_x * 2 + row_x) * capacity, capacity, block_len, sent_targets(inn_ref, 0, blocks)
    )
    batch_ref[mine, width:] = place(pick, pad_ref).astype(BF16)
    batch_ref[theirs, :width] = other_rows_ref[...]
    batch_ref[theirs, width:] = jnp.zeros((capacity, width), BF16)


VMEM = pl.BlockSpec(memory_space=pltpu.VMEM)
SMEM = pl.BlockSpec(memory_space=pltpu.SMEM)
HBM = pl.BlockSpec(memory_space=pltpu.HBM)
SDS = jax.ShapeDtypeStruct


def in_hbm(*arrays):
    return tuple(pltpu.with_memory_space_constraint(a, pltpu.HBM) for a in arrays)


def on_device(
    agents,
    block_fill,
    neighbours,
    target_slot,
    attention_in,
    attention_out,
    policy_in,
    policy_mid,
    policy_out,
):
    blocks_x, blocks_y, block_len, width = agents.shape
    all_blocks = blocks_x * blocks_y
    owners = lax.axis_size("gx")
    count_y = lax.axis_size("gy")
    row_x = lax.axis_index("gx")
    capacity = 3 * all_blocks * block_len // (4 * owners)
    hidden = policy_in.shape[1]
    acts = policy_out.shape[1]
    slots = all_blocks * LIVE
    half_rows = slots // 2
    rows = owners * capacity
    block_fill, neighbours = in_hbm(block_fill, neighbours)

    swap = [(0, 1), (1, 0)]
    across = [(i, i - 1) for i in range(2, count_y, 2)]
    across += [(i, i + 1) for i in range(1, count_y - 1, 2)]
    beside = [(i, i ^ 1) for i in range(count_y)]
    diagonal = [
        (g * count_y + a, (1 - g) * count_y + b) for g in range(owners) for a, b in across
    ]

    off, inn = pl.pallas_call(
        stage_kernel,
        out_shape=(SDS((half_rows, width), BF16), SDS((half_rows + TARGET_ROWS, width), BF16)),
        in_specs=[HBM, HBM],
        out_specs=(VMEM, VMEM),
        scratch_shapes=[
            pltpu.VMEM((blocks_x, blocks_y, block_len), jnp.int32),
            pltpu.SemaphoreType.DMA((3, blocks_x)),
        ],
        compiler_params=pltpu.CompilerParams(vmem_limit_bytes=4 * MIB),
        name="stage",
    )(*in_hbm(target_slot, agents))
    other_inn = lax.ppermute(inn, "gx", swap)
    other_off = lax.ppermute(off, "gx", swap)
    side_off = lax.ppermute(off, "gy", across)
    side_inn = lax.ppermute(inn, "gy", beside)
    other_side_off = lax.ppermute(off, ("gx", "gy"), diagonal)
    attention_in, attention_out, own_rows, pick_out, table, token = pl.pallas_call(
        local_kernel,
        out_shape=(
            SDS(attention_in.shape, BF16),
            SDS(attention_out.shape, BF16),
            SDS((capacity, width), BF16),
            SDS((capacity, all_blocks * block_len), BF16),
            SDS((all_blocks, 2 * neighbours.shape[2] + 2), jnp.int32),
            SDS((8, 128), F32),
        ),
        in_specs=[SMEM] * 2 + [VMEM] * 2 + [HBM] * 2,
        out_specs=(VMEM,) * 4 + (SMEM, VMEM),
        scratch_shapes=[
            pltpu.VMEM((all_blocks, block_len, width), BF16),
            pltpu.SemaphoreType.DMA((3,)),
        ],
        compiler_params=pltpu.CompilerParams(vmem_limit_bytes=8 * MIB),
        cost_estimate=pl.CostEstimate(
            flops=2 * capacity * all_blocks * block_len * width,
            bytes_accessed=8 * MIB,
            transcendentals=0,
        ),
        name="local",
    )(block_fill, neighbours, off, inn, *in_hbm(attention_in, attention_out))
    other_inn, side_off, other_off, side_inn, other_side_off, token = lax.optimization_barrier(
        (other_inn, side_off, other_off, side_inn, other_side_off, token)
    )
    other_side_inn = lax.ppermute(other_inn, "gy", beside)
    other_rows = pl.pallas_call(
        others_kernel,
        out_shape=SDS((capacity, width), BF16),
        in_specs=[VMEM, VMEM],
        out_specs=VMEM,
        scratch_shapes=[pltpu.VMEM((all_blocks, block_len, width), BF16)],
        compiler_params=pltpu.CompilerParams(vmem_limit_bytes=8 * MIB),
        cost_estimate=pl.CostEstimate(
            flops=2 * capacity * all_blocks * block_len * width,
            bytes_accessed=2 * MIB,
            transcendentals=0,
        ),
        name="others",
    )(other_off, other_inn)
    other_rows, other_side_inn = lax.optimization_barrier((other_rows, other_side_inn))

    window = blocks_x * owners * (blocks_y + 2 * REACH)
    scores = all_blocks * HEADS * LIVE * 5 * LIVE
    summary, packed = pl.pallas_call(
        attention_kernel,
        out_shape=(SDS((slots, width), BF16), SDS((capacity, width), BF16)),
        in_specs=[SMEM] + [VMEM] * 12,
        out_specs=(VMEM, VMEM),
        scratch_shapes=[
            pltpu.VMEM((window, LIVE, width), BF16),
            pltpu.VMEM((window, LIVE, width), BF16),
            pltpu.VMEM((slots, width), BF16),
            pltpu.VMEM((all_blocks, block_len, width), BF16),
        ],
        compiler_params=pltpu.CompilerParams(vmem_limit_bytes=16 * MIB),
        cost_estimate=pl.CostEstimate(
            flops=2 * (2 * scores + window * LIVE * 2 * width) * width,
            bytes_accessed=8 * MIB,
            transcendentals=2 * scores,
        ),
        name="attention",
    )(
        table,
        off,
        inn,
        other_off,
        other_inn,
        side_off,
        side_inn,
        other_side_off,
        other_side_inn,
        attention_in,
        attention_out,
        pick_out,
        token,
    )
    arrived = lax.ppermute(packed, "gx", swap)
    actions, batch = pl.pallas_call(
        policy_kernel,
        out_shape=(
            SDS((blocks_x, blocks_y, block_len, acts), BF16),
            SDS((rows, 2 * width), BF16),
        ),
        in_specs=[SMEM] + [VMEM] * 8,
        out_specs=(VMEM, VMEM),
        scratch_shapes=[
            pltpu.VMEM((slots, 2 * width), BF16),
            pltpu.VMEM((slots, hidden), BF16),
            pltpu.VMEM((slots, hidden), BF16),
            pltpu.VMEM((all_blocks, block_len, width), BF16),
        ],
        compiler_params=pltpu.CompilerParams(vmem_limit_bytes=16 * MIB),
        cost_estimate=pl.CostEstimate(
            flops=2 * slots * hidden * (2 * width + 2 * hidden + acts),
            bytes_accessed=12 * MIB,
            transcendentals=3 * slots * hidden,
        ),
        name="policy",
    )(
        table,
        off,
        inn,
        summary,
        own_rows,
        other_rows,
        policy_in,
        policy_mid,
        policy_out,
    )
    batch = lax.dynamic_update_slice(batch, arrived, ((1 - row_x) * capacity, width))
    return actions, batch.reshape(1, 1, rows, 2 * width)


def solution(mesh):
    return jax.shard_map(
        on_device,
        mesh=mesh,
        in_specs=(
            P("gx", "gy", None, None),
            P(),
            P("gx", "gy", None),
            P("gx", "gy", None),
            P(),
            P(),
            P(),
            P(),
            P(),
        ),
        out_specs=(P("gx", "gy", None, None), P("gx", "gy", None, None)),
        check_vma=False,
    )
```

```python
import math

import jax
import jax.numpy as jnp
from jax import lax
from jax.experimental import pallas as pl
from jax.experimental.pallas import tpu as pltpu
from jax.sharding import PartitionSpec as P

HEADS = 4
LIVE = 96
REACH = 2
SCORE_CAP = 30.0
NORM_EPS = 1e-06
LOG2_E = math.log2(math.e)
TARGET_ROWS = 8
MIB = 1 << 20
BF16 = jnp.bfloat16
F32 = jnp.float32


def nt_dot(a, b):
    return lax.dot_general(a, b, (((1,), (1,)), ((), ())), preferred_element_type=F32)


def key_tables(table_ref, fill_ref, near_ref, b, lx, ly, place):
    row_x, row_y, blocks_x, blocks_y = place
    rows_x, rows_y = fill_ref.shape
    columns = blocks_y + 2 * REACH
    key_blocks = near_ref.shape[2] + 1
    home_x = row_x * blocks_x + lx
    home_y = row_y * blocks_y + ly
    table_ref[b, 0] = lx * columns + ly + REACH
    table_ref[b, key_blocks] = fill_ref[home_x, home_y]
    for d in range(key_blocks - 1):
        direction = near_ref[lx, ly, d]
        cell = direction + jnp.where(direction >= 12, 1, 0)
        cell_x = (cell * 13) >> 6
        step_x = cell_x - REACH
        step_y = cell - cell_x * 5 - REACH
        at_x = home_x + step_x
        at_y = home_y + step_y
        inside = (at_x >= 0) & (at_x < rows_x) & (at_y >= 0) & (at_y < rows_y)
        safe_x = jnp.clip(at_x, 0, rows_x - 1)
        safe_y = jnp.clip(at_y, 0, rows_y - 1)
        tile_x = jnp.where(safe_x >= blocks_x, 1, 0)
        other = jnp.where(tile_x == row_x, 0, 1)
        in_x = safe_x - tile_x * blocks_x
        table_ref[b, 1 + d] = (other * blocks_x + in_x) * columns + ly + step_y + REACH
        table_ref[b, key_blocks + 1 + d] = jnp.where(inside, fill_ref[safe_x, safe_y], 0)


def one_hot(base, capacity, block_len, target_rows):
    row = lax.broadcasted_iota(jnp.int32, (capacity, block_len), 0) + base
    row = row.astype(F32)
    return jnp.concatenate(
        [jnp.where(row == target, 1.0, 0.0).astype(BF16) for target in target_rows], axis=1
    )


def place(pick, pad_ref):
    blocks, block_len, width = pad_ref.shape
    flat = pad_ref[...].reshape(blocks * block_len, width)
    return jnp.dot(pick, flat, preferred_element_type=F32)


def sent_targets(ref, first, count):
    start = ref.shape[0] - TARGET_ROWS
    half = ref.shape[1] // 2
    both = ref[start : start + TARGET_ROWS].astype(F32)
    rows = both[:, :half] * 256.0 + both[:, half:]
    return [rows[b : b + 1] for b in range(first, first + count)]


def spread(pad_ref, first, rows, blocks):
    _, block_len, width = pad_ref.shape
    for b in range(blocks):
        pad_ref[first + b, :LIVE] = rows[b * LIVE : (b + 1) * LIVE]
        pad_ref[first + b, LIVE:] = jnp.zeros((block_len - LIVE, width), pad_ref.dtype)


def stage_kernel(target_hbm, agents_hbm, off_ref, inn_ref, target_ref, sems):
    blocks_x, _, _, _ = agents_hbm.shape
    core = lax.axis_index("gy") & 1
    rows = REACH * LIVE
    targets = pltpu.make_async_copy(target_hbm, target_ref, sems.at[2, 0])
    targets.start()
    copies = []
    for x in range(blocks_x):
        for ref, column, s in ((off_ref, core * REACH, 0), (inn_ref, REACH - core * REACH, 1)):
            copies.append(
                pltpu.make_async_copy(
                    agents_hbm.at[x, pl.ds(column, REACH), pl.ds(0, LIVE)],
                    ref.at[pl.ds(x * rows, rows)].reshape(REACH, LIVE, ref.shape[1]),
                    sems.at[s, x],
                )
            )
    for copy in copies:
        copy.start()
    targets.wait()
    halves = []
    for column in (core * REACH, REACH - core * REACH):
        for x in range(blocks_x):
            for c in range(REACH):
                halves.append(target_ref[x, pl.ds(column + c, 1), :])
    target = jnp.concatenate(halves, axis=0)
    high = target >> 8
    low = target - high * 256
    split = jnp.concatenate([high, low], axis=1).astype(F32).astype(BF16)
    inn_ref[blocks_x * rows :] = split
    for copy in copies:
        copy.wait()


def local_kernel(
    fill_ref,
    near_ref,
    off_ref,
    inn_ref,
    weight_in_hbm,
    weight_out_hbm,
    weight_in_ref,
    weight_out_ref,
    own_rows_ref,
    pick_out_ref,
    table_ref,
    token_ref,
    pad_ref,
    sems,
):
    copies = [
        pltpu.make_async_copy(weight_in_hbm, weight_in_ref, sems.at[0]),
        pltpu.make_async_copy(weight_out_hbm, weight_out_ref, sems.at[1]),
    ]
    for copy in copies:
        copy.start()
    capacity = own_rows_ref.shape[0]
    blocks, block_len, _ = pad_ref.shape
    row_x = lax.axis_index("gx")
    core = lax.axis_index("gy") & 1
    place_of = (row_x, lax.axis_index("gy"), blocks // (2 * REACH), 2 * REACH)
    for half, first in enumerate((core * REACH, REACH - core * REACH)):
        for i in range(blocks // 2):
            b = half * (blocks // 2) + i
            at = (i // REACH, first + i % REACH)
            key_tables(table_ref, fill_ref, near_ref, b, *at, place_of)
    spread(pad_ref, 0, off_ref, blocks // 2)
    spread(pad_ref, blocks // 2, inn_ref, blocks // 2)
    targets = sent_targets(inn_ref, 0, blocks)
    pick_out_ref[...] = one_hot(
        ((1 - row_x) * 2 + row_x) * capacity, capacity, block_len, targets
    )
    pick = one_hot((row_x * 2 + row_x) * capacity, capacity, block_len, targets)
    own_rows_ref[...] = place(pick, pad_ref).astype(BF16)
    token_ref[...] = jnp.zeros_like(token_ref)
    for copy in copies:
        copy.wait()


def others_kernel(other_off_ref, other_inn_ref, other_rows_ref, pad_ref):
    capacity = other_rows_ref.shape[0]
    blocks, block_len, _ = pad_ref.shape
    row_x = lax.axis_index("gx")
    spread(pad_ref, 0, other_off_ref, blocks // 2)
    spread(pad_ref, blocks // 2, other_inn_ref, blocks // 2)
    pick = one_hot(
        (row_x * 2 + 1 - row_x) * capacity,
        capacity,
        block_len,
        sent_targets(other_inn_ref, 0, blocks),
    )
    other_rows_ref[...] = place(pick, pad_ref).astype(BF16)


def attention_kernel(
    table_ref,
    off_ref,
    inn_ref,
    other_off_ref,
    other_inn_ref,
    side_off_ref,
    side_inn_ref,
    other_side_off_ref,
    other_side_inn_ref,
    weight_in_ref,
    weight_out_ref,
    pick_out_ref,
    token_ref,
    summary_ref,
    packed_ref,
    keys_ref,
    values_ref,
    context_ref,
    pad_ref,
):
    width = weight_out_ref.shape[0]
    head = width // HEADS
    half_rows = off_ref.shape[0]
    each = half_rows // LIVE
    blocks_x = each // REACH
    columns = 4 * REACH
    core = lax.axis_index("gy") & 1
    at_off = REACH + REACH * core
    at_inn = 2 * REACH - REACH * core
    at_side_off = 3 * REACH * core
    at_side_inn = 3 * REACH - 3 * REACH * core
    sources = (
        (0, at_off, off_ref),
        (0, at_inn, inn_ref),
        (1, at_off, other_off_ref),
        (1, at_inn, other_inn_ref),
        (0, at_side_off, side_off_ref),
        (0, at_side_inn, side_inn_ref),
        (1, at_side_off, other_side_off_ref),
        (1, at_side_inn, other_side_inn_ref),
    )
    for s in range(0, len(sources), 4):
        group = sources[s : s + 4]
        rows = jnp.concatenate([ref[:half_rows] for _, _, ref in group], axis=0)
        both = jnp.dot(rows, weight_in_ref[:, width:], preferred_element_type=F32).astype(BF16)
        both = both.reshape(len(group) * each, LIVE, 2 * width)
        for g, (o, column, _) in enumerate(group):
            for x in range(blocks_x):
                at = (o * blocks_x + x) * columns + column
                first = g * each + x * REACH
                keys_ref[pl.ds(at, REACH)] = both[first : first + REACH, :, :width]
                values_ref[pl.ds(at, REACH)] = both[first : first + REACH, :, width:]

    key_blocks = table_ref.shape[1] // 2
    lane = lax.broadcasted_iota(jnp.int32, (1, key_blocks * LIVE), 1)
    head_of = lax.broadcasted_iota(jnp.int32, (1, width), 1) // head
    queries = [
        jnp.dot(ref[:half_rows], weight_in_ref[:, :width], preferred_element_type=F32).astype(BF16)
        for ref in (off_ref, inn_ref)
    ]
    for b in range(2 * each):
        where_to = [table_ref[b, j] for j in range(key_blocks)]
        counts = [table_ref[b, key_blocks + j] for j in range(key_blocks)]
        i = b % each
        query = queries[b // each][i * LIVE : (i + 1) * LIVE]
        split = jnp.concatenate(
            [jnp.where(head_of == h, query, jnp.zeros_like(query)) for h in range(HEADS)],
            axis=0,
        )
        keys = jnp.concatenate([keys_ref[w] for w in where_to], axis=0)
        values = jnp.concatenate([values_ref[w] for w in where_to], axis=0)
        end = jnp.full(lane.shape, counts[0], jnp.int32)
        for j in range(1, key_blocks):
            end = jnp.where(lane >= j * LIVE, counts[j] + j * LIVE, end)
        raw = nt_dot(split, keys)
        capped = jnp.tanh(raw * (1.0 / (math.sqrt(head) * SCORE_CAP)))
        weight = jnp.exp2(capped * (SCORE_CAP * LOG2_E))
        weight = jnp.where(lane < end, weight, 0.0)
        total = jnp.sum(weight, axis=-1, keepdims=True)
        weight = (weight * (1.0 / total)).astype(BF16)
        mixed = jnp.dot(weight, values, preferred_element_type=F32)
        context = mixed[:LIVE]
        for h in range(1, HEADS):
            context = jnp.where(head_of == h, mixed[h * LIVE : (h + 1) * LIVE], context)
        context_ref[b * LIVE : (b + 1) * LIVE] = context.astype(BF16)
    out = jnp.dot(context_ref[...], weight_out_ref[...], preferred_element_type=F32)
    scale = lax.rsqrt(jnp.mean(out * out, axis=-1, keepdims=True) + NORM_EPS)
    out = (out * scale).astype(BF16)
    summary_ref[...] = out
    spread(pad_ref, 0, out, 2 * each)
    packed_ref[...] = place(pick_out_ref[...], pad_ref).astype(BF16)


def silu(v):
    half = 0.5 * v
    return half + half * jnp.tanh(half)


def policy_kernel(
    table_ref,
    off_ref,
    inn_ref,
    summary_ref,
    own_rows_ref,
    other_rows_ref,
    policy_in_ref,
    policy_mid_ref,
    policy_out_ref,
    actions_ref,
    batch_ref,
    x_ref,
    h_ref,
    g_ref,
    pad_ref,
):
    width = off_ref.shape[1]
    blocks_x, blocks_y, block_len, _ = actions_ref.shape
    row_x = lax.axis_index("gx")
    core = lax.axis_index("gy") & 1
    capacity = batch_ref.shape[0] // 2
    half_rows = off_ref.shape[0]
    x_ref[:half_rows, :width] = off_ref[...]
    x_ref[half_rows:, :width] = inn_ref[:half_rows]
    x_ref[:, width:] = summary_ref[...]
    chunk = 256
    hidden = policy_in_ref.shape[1]
    for n in range(0, hidden, chunk):
        v = jnp.dot(x_ref[...], policy_in_ref[:, n : n + chunk], preferred_element_type=F32)
        h_ref[:, n : n + chunk] = silu(v).astype(BF16)
    now, later = h_ref, g_ref
    for m in range(policy_mid_ref.shape[0]):
        for n in range(0, hidden, chunk):
            v = jnp.dot(
                now[...], policy_mid_ref[m, :, n : n + chunk], preferred_element_type=F32
            )
            later[:, n : n + chunk] = silu(v).astype(BF16)
        now, later = later, now
    acts = jnp.dot(now[...], policy_out_ref[...], preferred_element_type=F32)
    slot = lax.broadcasted_iota(jnp.int32, (LIVE, 1), 0)
    for half, first in enumerate((core * REACH, REACH - core * REACH)):
        for i in range(blocks_x * REACH):
            lx = i // REACH
            ly = first + i % REACH
            b = half * blocks_x * REACH + i
            fill = table_ref[b, table_ref.shape[1] // 2]
            act = jnp.where(slot < fill, acts[b * LIVE : (b + 1) * LIVE], 0.0)
            actions_ref[lx, ly, :LIVE] = act.astype(BF16)
            actions_ref[lx, ly, LIVE:] = jnp.zeros((block_len - LIVE, act.shape[1]), BF16)

    mine = pl.ds(pl.multiple_of(row_x * capacity, capacity), capacity)
    theirs = pl.ds(pl.multiple_of((1 - row_x) * capacity, capacity), capacity)
    blocks = pad_ref.shape[0]
    batch_ref[mine, :width] = own_rows_ref[...]
    spread(pad_ref, 0, summary_ref, blocks)
    pick = one_hot(
        (row_x * 2 + row_x) * capacity, capacity, block_len, sent_targets(inn_ref, 0, blocks)
    )
    batch_ref[mine, width:] = place(pick, pad_ref).astype(BF16)
    batch_ref[theirs, :width] = other_rows_ref[...]
    batch_ref[theirs, width:] = jnp.zeros((capacity, width), BF16)


VMEM = pl.BlockSpec(memory_space=pltpu.VMEM)
SMEM = pl.BlockSpec(memory_space=pltpu.SMEM)
HBM = pl.BlockSpec(memory_space=pltpu.HBM)
SDS = jax.ShapeDtypeStruct


def in_hbm(*arrays):
    return tuple(pltpu.with_memory_space_constraint(a, pltpu.HBM) for a in arrays)


def on_device(
    agents,
    block_fill,
    neighbours,
    target_slot,
    attention_in,
    attention_out,
    policy_in,
    policy_mid,
    policy_out,
):
    blocks_x, blocks_y, block_len, width = agents.shape
    all_blocks = blocks_x * blocks_y
    owners = lax.axis_size("gx")
    count_y = lax.axis_size("gy")
    row_x = lax.axis_index("gx")
    capacity = 3 * all_blocks * block_len // (4 * owners)
    hidden = policy_in.shape[1]
    acts = policy_out.shape[1]
    slots = all_blocks * LIVE
    half_rows = slots // 2
    rows = owners * capacity
    block_fill, neighbours = in_hbm(block_fill, neighbours)

    swap = [(0, 1), (1, 0)]
    across = [(i, i - 1) for i in range(2, count_y, 2)]
    across += [(i, i + 1) for i in range(1, count_y - 1, 2)]
    beside = [(i, i ^ 1) for i in range(count_y)]
    diagonal = [
        (g * count_y + a, (1 - g) * count_y + b) for g in range(owners) for a, b in across
    ]

    off, inn = pl.pallas_call(
        stage_kernel,
        out_shape=(SDS((half_rows, width), BF16), SDS((half_rows + TARGET_ROWS, width), BF16)),
        in_specs=[HBM, HBM],
        out_specs=(VMEM, VMEM),
        scratch_shapes=[
            pltpu.VMEM((blocks_x, blocks_y, block_len), jnp.int32),
            pltpu.SemaphoreType.DMA((3, blocks_x)),
        ],
        compiler_params=pltpu.CompilerParams(vmem_limit_bytes=4 * MIB),
        name="stage",
    )(*in_hbm(target_slot, agents))
    other_inn = lax.ppermute(inn, "gx", swap)
    other_off = lax.ppermute(off, "gx", swap)
    side_off = lax.ppermute(off, "gy", across)
    side_inn = lax.ppermute(inn, "gy", beside)
    other_side_off = lax.ppermute(off, ("gx", "gy"), diagonal)
    attention_in, attention_out, own_rows, pick_out, table, token = pl.pallas_call(
        local_kernel,
        out_shape=(
            SDS(attention_in.shape, BF16),
            SDS(attention_out.shape, BF16),
            SDS((capacity, width), BF16),
            SDS((capacity, all_blocks * block_len), BF16),
            SDS((all_blocks, 2 * neighbours.shape[2] + 2), jnp.int32),
            SDS((8, 128), F32),
        ),
        in_specs=[SMEM] * 2 + [VMEM] * 2 + [HBM] * 2,
        out_specs=(VMEM,) * 4 + (SMEM, VMEM),
        scratch_shapes=[
            pltpu.VMEM((all_blocks, block_len, width), BF16),
            pltpu.SemaphoreType.DMA((3,)),
        ],
        compiler_params=pltpu.CompilerParams(vmem_limit_bytes=8 * MIB),
        cost_estimate=pl.CostEstimate(
            flops=2 * capacity * all_blocks * block_len * width,
            bytes_accessed=8 * MIB,
            transcendentals=0,
        ),
        name="local",
    )(block_fill, neighbours, off, inn, *in_hbm(attention_in, attention_out))
    other_inn, side_off, other_off, side_inn, other_side_off, token = lax.optimization_barrier(
        (other_inn, side_off, other_off, side_inn, other_side_off, token)
    )
    other_side_inn = lax.ppermute(other_inn, "gy", beside)
    other_rows = pl.pallas_call(
        others_kernel,
        out_shape=SDS((capacity, width), BF16),
        in_specs=[VMEM, VMEM],
        out_specs=VMEM,
        scratch_shapes=[pltpu.VMEM((all_blocks, block_len, width), BF16)],
        compiler_params=pltpu.CompilerParams(vmem_limit_bytes=8 * MIB),
        cost_estimate=pl.CostEstimate(
            flops=2 * capacity * all_blocks * block_len * width,
            bytes_accessed=2 * MIB,
            transcendentals=0,
        ),
        name="others",
    )(other_off, other_inn)
    other_rows, other_side_inn = lax.optimization_barrier((other_rows, other_side_inn))

    window = blocks_x * owners * (blocks_y + 2 * REACH)
    scores = all_blocks * HEADS * LIVE * 5 * LIVE
    summary, packed = pl.pallas_call(
        attention_kernel,
        out_shape=(SDS((slots, width), BF16), SDS((capacity, width), BF16)),
        in_specs=[SMEM] + [VMEM] * 12,
        out_specs=(VMEM, VMEM),
        scratch_shapes=[
            pltpu.VMEM((window, LIVE, width), BF16),
            pltpu.VMEM((window, LIVE, width), BF16),
            pltpu.VMEM((slots, width), BF16),
            pltpu.VMEM((all_blocks, block_len, width), BF16),
        ],
        compiler_params=pltpu.CompilerParams(vmem_limit_bytes=16 * MIB),
        cost_estimate=pl.CostEstimate(
            flops=2 * (2 * scores + window * LIVE * 2 * width) * width,
            bytes_accessed=8 * MIB,
            transcendentals=2 * scores,
        ),
        name="attention",
    )(
        table,
        off,
        inn,
        other_off,
        other_inn,
        side_off,
        side_inn,
        other_side_off,
        other_side_inn,
        attention_in,
        attention_out,
        pick_out,
        token,
    )
    arrived = lax.ppermute(packed, "gx", swap)
    actions, batch = pl.pallas_call(
        policy_kernel,
        out_shape=(
            SDS((blocks_x, blocks_y, block_len, acts), BF16),
            SDS((rows, 2 * width), BF16),
        ),
        in_specs=[SMEM] + [VMEM] * 8,
        out_specs=(VMEM, VMEM),
        scratch_shapes=[
            pltpu.VMEM((slots, 2 * width), BF16),
            pltpu.VMEM((slots, hidden), BF16),
            pltpu.VMEM((slots, hidden), BF16),
            pltpu.VMEM((all_blocks, block_len, width), BF16),
        ],
        compiler_params=pltpu.CompilerParams(vmem_limit_bytes=16 * MIB),
        cost_estimate=pl.CostEstimate(
            flops=2 * slots * hidden * (2 * width + 2 * hidden + acts),
            bytes_accessed=12 * MIB,
            transcendentals=3 * slots * hidden,
        ),
        name="policy",
    )(
        table,
        off,
        inn,
        summary,
        own_rows,
        other_rows,
        policy_in,
        policy_mid,
        policy_out,
    )
    batch = lax.dynamic_update_slice(batch, arrived, ((1 - row_x) * capacity, width))
    return actions, batch.reshape(1, 1, rows, 2 * width)


def solution(mesh):
    return jax.shard_map(
        on_device,
        mesh=mesh,
        in_specs=(
            P("gx", "gy", None, None),
            P(),
            P("gx", "gy", None),
            P("gx", "gy", None),
            P(),
            P(),
            P(),
            P(),
            P(),
        ),
        out_specs=(P("gx", "gy", None, None), P("gx", "gy", None, None)),
        check_vma=False,
    )
```
